256 devices in a mesh: row: 16 (over z, core), col: 16 (over x, y).
Axes of the slice: x: 4, y: 4, z: 8, core: 2. Of those that a mesh axis runs over, the one named last changes fastest.
Arguments:
- inputs: bfloat16 [4096, 18432], P('col', 'row'), may hold values from -6 to 6
- out_grads: bfloat16 [4096, 18432], P('row', 'col'), may hold values from -0.09375 to 0.09375
- range_test: float32 [18432, 128], P('col'), may hold values from -0.046875 to 0.046875
- corange_test: float32 [256, 18432], P(None, 'row'), may hold values from -0.046875 to 0.046875
Outputs:
- range_sketch: float32 [18432, 128], P('row')
- corange_sketch: float32 [256, 18432], P(None, 'col')
- residual: float32 [18432, 18432], P('row', 'col')
The draws below stay inside these ranges and needn't reach their ends.
All inputs are finite; a program needn't handle non-finite values.
Results may differ from the reference program's by a relative error of at most 0.0003.
Values may be sent and summed in bfloat16 or wider, within the bound.
A program may use at most 128 MiB of HBM per device.

```python
import jax
import jax.numpy as jnp
from jax import lax

M = 18432
N = 18432
RANK_Y = 128
RANK_Z = 256
TOKENS = 4096


def levels(stream_key, shape, cuts, low, largest):
    def one(axis_at, shards_of):
        steps = jax.random.uniform(jax.random.fold_in(jax.random.fold_in(stream_key, 6), axis_at), (shards_of,), jnp.float32, low / len(cuts), largest / len(cuts))
        return jnp.repeat(jnp.exp(steps), shape[axis_at] // shards_of).reshape((-1,) + (1,) * (len(shape) - axis_at - 1))

    factor_of = one(*cuts[0])
    for cut in cuts[1:]:
        factor_of = factor_of * one(*cut)
    return factor_of


def bell_draw(own_key, dims, scale, most, split=(), kind=jnp.bfloat16):
    factor_of = levels(own_key, dims, split, -0.22, 0.18) if split else 1.0
    array = jax.random.normal(own_key, dims, jnp.float32) * scale * factor_of
    return jnp.minimum(jnp.maximum(array, -most), most).astype(kind)


def setup_inputs(seed: int = 0) -> dict:
    arg_keys = jax.random.split(jax.random.key(seed), 5)
    return {
        "inputs": bell_draw(arg_keys[0], (TOKENS, M), 1.0, 6.0, ((0, 16), (1, 16))),
        "out_grads": bell_draw(arg_keys[1], (TOKENS, N), TOKENS ** -0.5, 0.09375, ((0, 16), (1, 16))),
        "range_test": bell_draw(arg_keys[2], (N, RANK_Y), N ** -0.5, 0.046875, ((0, 16),), jnp.float32),
        "corange_test": bell_draw(arg_keys[3], (RANK_Z, M), M ** -0.5, 0.046875, ((1, 16),), jnp.float32),
    }


def reference(inputs, out_grads, range_test, corange_test):
    highest = lax.Precision.HIGHEST
    gradient = lax.dot_general(inputs.astype(jnp.float32), out_grads.astype(jnp.float32), (((0,), (0,)), ((), ())), preferred_element_type=jnp.float32)
    range_sketch = jnp.dot(gradient.astype(jnp.float32), range_test.astype(jnp.float32), precision=highest, preferred_element_type=jnp.float32)
    corange_sketch = jnp.dot(corange_test.astype(jnp.float32), gradient.astype(jnp.float32), precision=highest, preferred_element_type=jnp.float32)
    core_input = jnp.dot(corange_test.astype(jnp.float32), range_sketch.astype(jnp.float32), precision=highest, preferred_element_type=jnp.float32)
    gram_matrix = jnp.dot(core_input.T.astype(jnp.float32), core_input.astype(jnp.float32), precision=highest, preferred_element_type=jnp.float32)
    factor_low = jnp.linalg.cholesky(gram_matrix)
    core_map = jax.scipy.linalg.cho_solve((factor_low, True), core_input.T)
    project = jnp.dot(core_map.astype(jnp.float32), corange_sketch.astype(jnp.float32), precision=highest, preferred_element_type=jnp.float32)
    residual = gradient - jnp.dot(range_sketch.astype(jnp.float32), project.astype(jnp.float32), precision=highest, preferred_element_type=jnp.float32)
    return (range_sketch, corange_sketch, residual)
```

```python
import jax
import jax.numpy as jnp
from jax import lax
from jax.experimental import pallas as pl
from jax.experimental.pallas import tpu as pltpu
from jax.sharding import PartitionSpec as P

F32 = jnp.float32
BF16 = jnp.bfloat16
HIGHEST = lax.Precision.HIGHEST
MESH = pl.DeviceIdType.MESH

BLOCK = 1152
TOK = 256
UNIT = 288
COLS = 384
RY = 128
RZ = 256


def dot(left_side, right_side, precision=None):
    return jnp.dot(left_side, right_side, precision=precision, preferred_element_type=F32)


def split(value, parts):
    out = []
    for _ in range(parts):
        piece = value.astype(BF16)
        value = value - piece.astype(F32)
        out.append(piece)
    return out


def exchange_kernel(
    xt_ref, y_ref, om_ref, psi_ref,
    q_ref, p_ref, r_ref, g_hbm,
    xt4, yf, af, wf, ahl, whl, g_acc, a_part, w_part, a_in, w_in, inv_ref,
    rs_send, rs_recv, ag_send, ag_recv, ring_send, ring_recv, prt_send, prt_recv,
    z_send, z_recv, yp_send, yp_recv, own_send, own_recv, local_sem, g_sem,
):
    row, col = lax.axis_index("row"), lax.axis_index("col")
    z, k = row // 2, row % 2
    x, y = col // 4, col % 4
    partner = row + 1 - 2 * k

    barrier = pltpu.get_barrier_semaphore()

    def greet(j, carry):
        pl.semaphore_signal(barrier, inc=1, device_id=((row + j) % 16, col), device_id_type=MESH)
        pl.semaphore_signal(barrier, inc=1, device_id=(row, (col + j) % 16), device_id_type=MESH)
        return carry

    lax.fori_loop(1, 16, greet, 0)

    def own_left(i, carry):
        rows = pl.ds(pl.multiple_of(i * 128, 128), 128)
        parts = jnp.concatenate(split(psi_ref[rows, :], 3), axis=0)
        both = dot(parts, xt_ref[...])
        total = both[0:128] + both[128:256] + both[256:384]
        a_part[pl.ds(pl.multiple_of(i * 8, 8), 8)] = total.reshape(8, 16, TOK)
        return carry

    lax.fori_loop(0, 2, own_left, 0)
    parts = jnp.concatenate(split(om_ref[...], 3), axis=1)
    both = dot(y_ref[...], parts)
    w_part[...] = (both[:, 0:128] + both[:, 128:256] + both[:, 256:384]).reshape(16, 16, RY)

    pl.semaphore_wait(barrier, 30)

    def remote(source, target, send, recv, device):
        return pltpu.make_async_remote_copy(
            src_ref=source, dst_ref=target, send_sem=send, recv_sem=recv,
            device_id=device, device_id_type=MESH,
        )

    me_row = 8 * k + z

    def rs_left(t):
        slot = 8 * (t % 2) + t // 2
        return remote(a_part.at[slot], a_in.at[me_row], rs_send.at[0, slot], rs_recv.at[0, me_row], (t, col))

    def rs_right(t):
        return remote(w_part.at[t], w_in.at[col], rs_send.at[1, t], rs_recv.at[1, col], (row, t))

    def rs_start(j, carry):
        rs_left((row + j) % 16).start()
        rs_right((col + j) % 16).start()
        return carry

    lax.fori_loop(1, 16, rs_start, 0)

    def view(p, v, first, second):
        xi, yi = (first, second) if v < 2 else (second, first)
        if p == 0:
            return xt4.at[xi, yi, pl.ds(UNIT * v, UNIT), :]
        if p == 1:
            return af.at[xi, yi, k, pl.ds(2 * v, 2)]
        return wf.at[xi, yi, k, pl.ds(2 * v, 2)]

    def axes(v):
        return (x, y) if v < 2 else (y, x)

    def neighbour(v, phase, step):
        along_x = (v < 2) == (phase == 0)
        if along_x:
            return (row, ((x + step + 4) % 4) * 4 + y)
        return (row, x * 4 + (y + step + 4) % 4)

    def ring_view(p, v, phase, offset):
        first, second = axes(v)
        if phase == 0:
            return view(p, v, (first + offset + 4) % 4, second)
        return view(p, v, slice(None), (second + offset + 4) % 4)

    def ring_send_copy(p, v, phase, j):
        far = 1 if v % 2 == 0 else -1
        step = (1, -1, far)[j]
        offset = (0, 0, -far)[j]
        here = ring_view(p, v, phase, offset)
        return remote(
            here, here, ring_send.at[p, v, phase, j], ring_recv.at[p, v, phase, j], neighbour(v, phase, step)
        )

    def ring_start(p, v, phase):
        ring_send_copy(p, v, phase, 0).start()
        ring_send_copy(p, v, phase, 1).start()

    def ring_wait(p, v, phase, j):
        there = ring_view(p, v, phase, (-1, 1, 2)[j])
        remote(
            there, there, ring_send.at[p, v, phase, j], ring_recv.at[p, v, phase, j], neighbour(v, phase, 1)
        ).wait_recv()

    def partner_copy(p, v, phase, j):
        there = ring_view(p, v, phase, (-1, 1, 2)[j])
        return remote(
            there, there, prt_send.at[p, v, phase, j], prt_recv.at[p, v, phase, j], (partner, col)
        )

    def ring_near(p, v, phase):
        far = 0 if v % 2 == 0 else 1
        for j in (far, 1 - far):
            ring_wait(p, v, phase, j)
            if j == far:
                ring_send_copy(p, v, phase, 2).start()
            if p:
                partner_copy(p, v, phase, j).start()

    def ring_far(p, v, phase):
        ring_wait(p, v, phase, 2)
        if p:
            partner_copy(p, v, phase, 2).start()

    def z_view(h, offset):
        return yf.at[2 * ((z + offset + 8) % 8) + k, :, pl.ds(COLS * h, COLS)]

    def z_copy(h, d, s):
        step = 1 if d == 0 else -1
        here = z_view(h, -s * step)
        return remote(here, here, z_send.at[h, d, s], z_recv.at[h, d, s], (2 * ((z + step + 8) % 8) + k, col))

    def z_long(h, d):
        return (h % 2) == d

    def yp_copy(h, d, s):
        here = z_view(h, -s if d == 0 else s)
        return remote(here, here, yp_send.at[h, d, s], yp_recv.at[h, d, s], (partner, col))

    def z_own(h):
        z_copy(h, 0, 0).start()
        z_copy(h, 1, 0).start()
        yp_copy(h, 0, 0).start()

    def z_event(h, s):
        for d in (0, 1):
            if s == 4 and not z_long(h, d):
                continue
            step = 1 if d == 0 else -1
            here = z_view(h, -s * step)
            remote(here, here, z_send.at[h, d, s - 1], z_recv.at[h, d, s - 1], (partner, col)).wait_recv()
            if s < 3 or (s == 3 and z_long(h, d)):
                z_copy(h, d, s).start()
            yp_copy(h, d, s).start()

    own_x = pltpu.make_async_copy(xt_ref, xt4.at[x, y], local_sem.at[0])
    own_y = pltpu.make_async_copy(y_ref, yf.at[row], local_sem.at[1])
    own_x.start()
    own_y.start()
    own_x.wait()
    own_y.wait()
    for v in range(4):
        ring_start(0, v, 0)
    z_own(0)

    def rs_done(j, carry):
        t, c = (row + j) % 16, (col + j) % 16
        slot = 8 * (t % 2) + t // 2
        remote(a_part.at[slot], a_in.at[slot], rs_send.at[0, slot], rs_recv.at[0, slot], (t, col)).wait()
        remote(w_part.at[c], w_in.at[c], rs_send.at[1, c], rs_recv.at[1, c], (row, c)).wait()
        return carry

    lax.fori_loop(1, 16, rs_done, 0)

    def rs_sum(j, carry):
        left, right = carry
        t, c = (row + j) % 16, (col + j) % 16
        slot = 8 * (t % 2) + t // 2
        return left + a_in[slot], right + w_in[c]

    left, right = lax.fori_loop(1, 16, rs_sum, (a_part[me_row], w_part[col]))
    af[x, y, k, z] = left
    wf[x, y, k, z] = right
    z_own(1)

    def ag_copy(p, t):
        here = af.at[x, y, k, z] if p == 0 else wf.at[x, y, k, z]
        return remote(here, here, ag_send.at[p, t], ag_recv.at[p, z], (2 * t + k, col))

    def ag_start(j, carry):
        t = (z + j) % 8
        ag_copy(0, t).start()
        ag_copy(1, t).start()
        return carry

    lax.fori_loop(1, 8, ag_start, 0)

    for v in (0, 2, 1, 3):
        ring_near(0, v, 0)
    z_event(0, 1)
    for v in (0, 2):
        ring_far(0, v, 0)
        ring_start(0, v, 1)

    def ag_done(j, carry):
        t = (z + j) % 8
        for p, buffer in enumerate((af, wf)):
            there = buffer.at[x, y, k, t]
            remote(there, there, ag_send.at[p, t], ag_recv.at[p, t], (2 * t + k, col)).wait_recv()
        return carry

    lax.fori_loop(1, 8, ag_done, 0)
    for v in range(4):
        for p in (1, 2):
            ring_start(p, v, 0)
    own_half = []
    for p, buffer in enumerate((af, wf)):
        half = buffer.at[x, y, k]
        copy = remote(half, half, own_send.at[p], own_recv.at[p], (partner, col))
        copy.start()
        own_half.append(copy)

    z_event(1, 1)
    z_event(0, 2)
    for v in range(4):
        for p in (1, 2):
            ring_near(p, v, 0)
    z_event(1, 2)
    z_own(2)
    for v in range(4):
        for p in (1, 2):
            ring_far(p, v, 0)
            ring_start(p, v, 1)
    for v in (1, 3):
        ring_far(0, v, 0)
    for v in (0, 2):
        ring_near(0, v, 1)
    z_event(0, 3)
    for v in (1, 3):
        ring_start(0, v, 1)
    z_event(1, 3)
    for v in range(4):
        for p in (1, 2):
            ring_near(p, v, 1)
    z_event(0, 4)
    z_event(1, 4)
    for v in range(4):
        for p in (1, 2):
            ring_far(p, v, 1)
    z_event(2, 1)

    for p, buffer in enumerate((af, wf)):
        half = buffer.at[x, y, 1 - k]
        remote(half, half, own_send.at[p], own_recv.at[p], (partner, col)).wait_recv()
    for p in (1, 2):
        buffer = (af, wf)[p - 1]
        for v in range(4):
            first, second = axes(v)
            for phase in (0, 1):
                for j in range(3):
                    offset = (-1, 1, 2)[j]
                    if phase == 0:
                        f, s = (first + offset + 4) % 4, second
                    else:
                        f, s = slice(None), (second + offset + 4) % 4
                    xi, yi = (f, s) if v < 2 else (s, f)
                    there = buffer.at[xi, yi, 1 - k, pl.ds(2 * v, 2)]
                    remote(
                        there, there, prt_send.at[p, v, phase, j], prt_recv.at[p, v, phase, j], (partner, col)
                    ).wait_recv()

    z_event(2, 2)

    def core_step(b, core):
        left = af[b // 4, b % 4].reshape(RZ, TOK)
        right = wf[:, :, b % 2, b // 2].reshape(TOK, RY)
        ahl[b] = jnp.concatenate(split(left, 2), axis=0)
        whl[b] = jnp.concatenate(split(right, 2), axis=1)
        return core + dot(left, right, HIGHEST)

    core = lax.fori_loop(0, 16, core_step, jnp.zeros((RZ, RY), F32))
    z_event(2, 3)
    core_t = core.T
    inv_ref[...] = dot(core_t, core, HIGHEST)
    lanes = lax.broadcasted_iota(jnp.int32, (RY, RY), 1)
    subs = lax.broadcasted_iota(jnp.int32, (RY, RY), 0)

    def pivot(i, carry):
        now = inv_ref[...]
        line = inv_ref[pl.ds(i, 1), :]
        at_lane = lanes == i
        across = jnp.sum(jnp.where(at_lane, now, 0.0), axis=1, keepdims=True)
        head = jnp.sum(jnp.where(at_lane[0:1], line, 0.0), axis=1, keepdims=True)
        scaled = line / head
        inner = now - across * scaled
        on_line = jnp.where(at_lane, 1.0 / head, scaled)
        off_line = jnp.where(at_lane, -across / head, inner)
        inv_ref[...] = jnp.where(subs == i, on_line, off_line)
        return carry

    lax.fori_loop(0, RY, pivot, 0)
    core_map = dot(inv_ref[...], core_t, HIGHEST)

    z_event(2, 4)
    for v in (1, 3):
        ring_near(0, v, 1)
    for v in (0, 2, 1, 3):
        ring_far(0, v, 1)

    for h in range(3):
        for d in (0, 1):
            for s in range(5):
                if (s == 0 and d == 1) or (s == 4 and not z_long(h, d)):
                    continue
                offset = -s if d == 0 else s
                there = yf.at[2 * ((z + offset + 8) % 8) + 1 - k, :, pl.ds(COLS * h, COLS)]
                remote(there, there, yp_send.at[h, d, s], yp_recv.at[h, d, s], (partner, col)).wait_recv()

    def unit_rows(u):
        rows = pl.ds(pl.multiple_of(u * UNIT, 32), UNIT)
        return jnp.concatenate([xt4[b // 4, b % 4, rows, :] for b in range(16)], axis=1)

    def right_step(u, carry):
        rows = pl.ds(pl.multiple_of(u * UNIT, 32), UNIT)
        both = dot(unit_rows(u), whl[...].reshape(16 * TOK, 2 * RY))
        q_ref[rows, :] = both[:, 0:RY] + both[:, RY:]
        return carry

    lax.fori_loop(0, 4, right_step, 0)

    def left_step(h, carry):
        cols = pl.ds(pl.multiple_of(h * COLS, 128), COLS)
        lhs = jnp.concatenate([ahl[b] for b in range(16)], axis=1)
        both = dot(lhs, yf[:, :, cols].reshape(16 * TOK, COLS))
        total = both[0:RZ] + both[RZ:]
        p_ref[:, cols] = total
        r_ref[:, cols] = dot(core_map, total, HIGHEST)
        return carry

    lax.fori_loop(0, 3, left_step, 0)

    def tile_step(i, carry):
        u, h = i // 3, i % 3
        rows = pl.ds(pl.multiple_of(u * UNIT, 32), UNIT)
        cols = pl.ds(pl.multiple_of(h * COLS, 128), COLS)
        g_acc[rows, cols] = dot(unit_rows(u), yf[:, :, cols].reshape(16 * TOK, COLS))
        return carry

    lax.fori_loop(0, 12, tile_step, 0)
    out = pltpu.make_async_copy(g_acc, g_hbm, g_sem)
    out.start()

    def ag_sent(j, carry):
        t = (z + j) % 8
        ag_copy(0, t).wait_send()
        ag_copy(1, t).wait_send()
        return carry

    lax.fori_loop(1, 8, ag_sent, 0)
    for copy in own_half:
        copy.wait_send()
    for v in range(4):
        for phase in (0, 1):
            for j in range(3):
                for p in range(3):
                    ring_send_copy(p, v, phase, j).wait_send()
                    if p:
                        partner_copy(p, v, phase, j).wait_send()
    for h in range(3):
        for d in (0, 1):
            for s in range(5):
                if s < 3 or (s == 3 and z_long(h, d)):
                    z_copy(h, d, s).wait_send()
                if (s == 0 and d == 1) or (s == 4 and not z_long(h, d)):
                    continue
                yp_copy(h, d, s).wait_send()
    out.wait()


def exchange(xt, y, om, psi):
    dma = pltpu.SemaphoreType.DMA
    return pl.pallas_call(
        exchange_kernel,
        name="exchange",
        out_shape=(
            jax.ShapeDtypeStruct((BLOCK, RY), F32),
            jax.ShapeDtypeStruct((RZ, BLOCK), F32),
            jax.ShapeDtypeStruct((RY, BLOCK), F32),
            jax.ShapeDtypeStruct((BLOCK, BLOCK), F32),
        ),
        in_specs=[pl.BlockSpec(memory_space=pltpu.VMEM)] * 4,
        out_specs=(
            pl.BlockSpec(memory_space=pltpu.VMEM),
            pl.BlockSpec(memory_space=pltpu.VMEM),
            pl.BlockSpec(memory_space=pltpu.VMEM),
            pl.BlockSpec(memory_space=pl.ANY),
        ),
        scratch_shapes=[
            pltpu.VMEM((4, 4, BLOCK, TOK), BF16),
            pltpu.VMEM((16, TOK, BLOCK), BF16),
            pltpu.VMEM((4, 4, 2, 8, 16, TOK), F32),
            pltpu.VMEM((4, 4, 2, 8, 16, RY), F32),
            pltpu.VMEM((16, 2 * RZ, TOK), BF16),
            pltpu.VMEM((16, TOK, 2 * RY), BF16),
            pltpu.VMEM((BLOCK, BLOCK), F32),
            pltpu.VMEM((16, 16, TOK), F32),
            pltpu.VMEM((16, 16, RY), F32),
            pltpu.VMEM((16, 16, TOK), F32),
            pltpu.VMEM((16, 16, RY), F32),
            pltpu.VMEM((RY, RY), F32),
            dma((2, 16)), dma((2, 16)),
            dma((2, 8)), dma((2, 8)),
            dma((3, 4, 2, 3)), dma((3, 4, 2, 3)),
            dma((3, 4, 2, 3)), dma((3, 4, 2, 3)),
            dma((3, 2, 4)), dma((3, 2, 4)),
            dma((3, 2, 5)), dma((3, 2, 5)),
            dma((2,)), dma((2,)),
            dma((2,)), dma,
        ],
        compiler_params=pltpu.CompilerParams(
            collective_id=0, has_side_effects=True, vmem_limit_bytes=62 * 1024 * 1024
        ),
    )(xt, y, om, psi)


def finish_kernel(g_ref, q_ref, r_ref, p_ref, res_ref, qo_ref, po_ref):
    q_high, q_low = split(q_ref[...], 2)
    r_high, r_low = split(r_ref[...], 2)
    left = jnp.concatenate([q_high, q_low, q_high], axis=1)
    right = jnp.concatenate([r_high, r_high, r_low], axis=0)
    res_ref[...] = g_ref[...] - dot(left, right)
    qo_ref[...] = q_ref[...]
    po_ref[...] = p_ref[...]


def finish(g, q, r, p):
    steps = 8
    rows, prows = BLOCK // steps, RZ // steps
    return pl.pallas_call(
        finish_kernel,
        name="finish",
        grid=(steps,),
        out_shape=(
            jax.ShapeDtypeStruct((BLOCK, BLOCK), F32),
            jax.ShapeDtypeStruct((BLOCK, RY), F32),
            jax.ShapeDtypeStruct((RZ, BLOCK), F32),
        ),
        in_specs=[
            pl.BlockSpec((rows, BLOCK), lambda i: (i, 0)),
            pl.BlockSpec((rows, RY), lambda i: (i, 0)),
            pl.BlockSpec((RY, BLOCK), lambda i: (0, 0)),
            pl.BlockSpec((prows, BLOCK), lambda i: (i, 0)),
        ],
        out_specs=(
            pl.BlockSpec((rows, BLOCK), lambda i: (i, 0)),
            pl.BlockSpec((rows, RY), lambda i: (i, 0)),
            pl.BlockSpec((prows, BLOCK), lambda i: (i, 0)),
        ),
    )(g, q, r, p)


def per_device(inputs, out_grads, range_test, corange_test):
    q, p, r, g = exchange(inputs.T, out_grads, range_test, corange_test)
    residual, q, p = finish(g, q, r, p)
    return (q, p, residual)


def solution(mesh):
    placed = (P("col", "row"), P("row", "col"), P("col", None), P(None, "row"))
    return jax.shard_map(
        per_device,
        mesh=mesh,
        in_specs=placed,
        out_specs=(P("row", None), P(None, "col"), P("row", "col")),
        check_vma=False,
    )
```

```python
import heapq

import jax
import jax.numpy as jnp
from jax import lax
from jax.experimental import pallas as pl
from jax.experimental.pallas import tpu as pltpu
from jax.sharding import PartitionSpec as P

F32 = jnp.float32
BF16 = jnp.bfloat16
HIGHEST = lax.Precision.HIGHEST
MESH = pl.DeviceIdType.MESH

BLOCK = 1152
TOK = 256
RY = 128
RZ = 256
UNITS = (384, 384, 256, 128)
CHUNKS = (512, 512, 128)
FINISH_COLS = 384

LINK_RATE = 46500.0
PARTNER_RATE = 150000.0
HOP = 1.6
SLACK = 2.5


def starts(sizes):
    return [sum(sizes[:i]) for i in range(len(sizes))]


UNIT_AT = starts(UNITS)
CHUNK_AT = starts(CHUNKS)


def dot(left_side, right_side, precision=None):
    return jnp.dot(left_side, right_side, precision=precision, preferred_element_type=F32)


def split(value, parts):
    out = []
    for _ in range(parts):
        piece = value.astype(BF16)
        value = value - piece.astype(F32)
        out.append(piece)
    return out


class Message:
    def __init__(self, name, loads, order, start, wait, then=None, sent=None, latency=HOP):
        self.name, self.loads, self.order = name, loads, order
        self.start, self.wait, self.then, self.sent, self.latency = start, wait, then, sent, latency


class Plan:
    def __init__(self):
        self.now, self.free, self.queues = 0.0, {}, {}
        self.flying, self.count, self.done, self.tasks, self.sent = [], 0, set(), [], []

    def post(self, message):
        self.count += 1
        link = next(iter(message.loads))
        heapq.heappush(self.queues.setdefault(link, []), (message.order, self.count, message))

    def launch(self, message):
        message.start()
        self.now += 0.03
        end = self.now
        for link, cost in message.loads.items():
            self.free[link] = max(self.now, self.free.get(link, 0.0)) + cost
            end = max(end, self.free[link])
        self.count += 1
        heapq.heappush(self.flying, (end + message.latency, self.count, message))
        if message.sent:
            self.sent.append(message.sent)

    def poll(self):
        for link, queue in self.queues.items():
            while queue and self.free.get(link, 0.0) - self.now < SLACK:
                self.launch(heapq.heappop(queue)[2])

    def task(self, name, needs, order, cost, run):
        self.tasks.append((order, len(self.tasks), name, frozenset(needs), cost, run))

    def finish(self, name):
        self.done.add(name)

    def run(self, log=None):
        while True:
            self.poll()
            if self.flying and self.flying[0][0] <= self.now:
                message = heapq.heappop(self.flying)[2]
                message.wait()
                if log is not None:
                    log.append((round(self.now, 1), "recv", message.name))
                self.now += 0.03
                self.finish(message.name)
                if message.then:
                    message.then()
                continue
            ready = [task for task in self.tasks if task[3] <= self.done]
            if ready:
                best = min(ready)
                self.tasks.remove(best)
                if log is not None:
                    log.append((round(self.now, 1), "task", best[2]))
                best[5]()
                self.now += best[4]
                self.finish(best[2])
                continue
            if not self.flying:
                break
            self.now = self.flying[0][0]
        assert not self.tasks, [(task[2], task[3] - self.done) for task in self.tasks]


def exchange_kernel(
    x_hbm, y_hbm, om_hbm, psi_hbm,
    q_ref, r_ref, p_hbm, g_hbm,
    xt4, yf, wf, ar, ahl, whl, g_acc, p_all, c_all, map_ref,
    x_own, om, psi, a_part, w_part, a_in, w_in, inv_ref,
    rs_send, rs_recv, ga_send, ga_recv, gw_send, gw_recv, gc_send, gc_recv, gp_send, gp_recv,
    x_send, x_recv, w_send, w_recv, wp_send, wp_recv,
    z_send, z_recv, yp_send, yp_recv, p_send, p_recv, pp_send, pp_recv,
    own_send, own_recv, local_sem, out_sem,
):
    row, col = lax.axis_index("row"), lax.axis_index("col")
    z, k = row // 2, row % 2
    x, y = col // 4, col % 4
    partner = row + 1 - 2 * k
    me_row = 8 * k + z

    loads_in = [
        pltpu.make_async_copy(x_hbm, x_own, local_sem.at[0]),
        pltpu.make_async_copy(y_hbm, yf.at[row], local_sem.at[1]),
        pltpu.make_async_copy(psi_hbm, psi, local_sem.at[2]),
        pltpu.make_async_copy(om_hbm, om, local_sem.at[3]),
    ]
    for copy in loads_in:
        copy.start()

    barrier = pltpu.get_barrier_semaphore()

    def greet(j, carry):
        pl.semaphore_signal(barrier, inc=1, device_id=((row + j) % 16, col), device_id_type=MESH)
        pl.semaphore_signal(barrier, inc=1, device_id=(row, (col + j) % 16), device_id_type=MESH)
        return carry

    lax.fori_loop(1, 16, greet, 0)

    def remote(source, target, send, recv, device):
        return pltpu.make_async_remote_copy(
            src_ref=source, dst_ref=target, send_sem=send, recv_sem=recv,
            device_id=device, device_id_type=MESH,
        )

    plan = Plan()

    def along(first_axis, step):
        if first_axis:
            return (row, ((x + step + 4) % 4) * 4 + y)
        return (row, x * 4 + (y + step + 4) % 4)

    def x_view(u, a, o1, o2):
        n = UNITS[u] // 2
        rows = pl.ds(UNIT_AT[u] + n * a, n)
        ox, oy = (o1, o2) if a == 0 else (o2, o1)
        return xt4.at[(x + ox + 4) % 4, (y + oy + 4) % 4, rows, :]

    def x_message(u, a, phase, o1, step, hop):
        on_x = (a == 0) == (phase == 0)
        link = ("x" if on_x else "y") + ("+" if step > 0 else "-")
        if phase == 0:
            slot = {(1, 1): 0, (-1, 1): 1}.get((step, hop), 2)
            out_o, in_o = (-step * (hop - 1), 0), (-step * hop, 0)
        else:
            slot = 3 + 3 * (o1 % 4) + {(1, 1): 0, (-1, 1): 1}.get((step, hop), 2)
            out_o, in_o = (o1, -step * (hop - 1)), (o1, -step * hop)
        here, there = x_view(u, a, *out_o), x_view(u, a, *in_o)
        send, recv = x_send.at[u, a, slot], x_recv.at[u, a, slot]
        name = ("x", u, a, slot)

        def start():
            remote(here, here, send, recv, along(on_x, step)).start()

        def wait():
            remote(there, there, send, recv, along(on_x, step)).wait_recv()

        def sent():
            remote(here, here, send, recv, along(on_x, step)).wait_send()

        def then():
            if phase == 0:
                far = 1 if (u + a) % 2 == 0 else -1
                if hop == 1 and step == far:
                    plan.post(x_message(u, a, 0, 0, step, 2))
                came = (-step * hop) % 4
                plan.post(x_message(u, a, 1, came, 1, 1))
                plan.post(x_message(u, a, 1, came, -1, 1))
            else:
                far = 1 if (o1 % 4 in (0, 2)) == ((u + a) % 2 == 0) else -1
                if hop == 1 and step == far:
                    plan.post(x_message(u, a, 1, o1, step, 2))

        cost = UNITS[u] // 2 * TOK * 2 / LINK_RATE
        return Message(name, {link: cost}, (1, u, phase), start, wait, then, sent)

    def x_names(u):
        return [("x", u, a, slot) for a in (0, 1) for slot in range(15)]

    def x_begin(u):
        for a in (0, 1):
            for phase in (0, 1):
                for step in (1, -1):
                    plan.post(x_message(u, a, phase, 0, step, 1))

    def ring_long(h, d):
        return (h % 2) == d

    def z_peer(step):
        return (2 * ((z + step + 8) % 8) + k, col)

    def y_view(h, offset, kk):
        return yf.at[2 * ((z + offset + 8) % 8) + kk, :, pl.ds(CHUNK_AT[h], CHUNKS[h])]

    def p_view(h, offset, kk):
        return p_all.at[kk, (z + offset + 8) % 8, :, pl.ds(CHUNK_AT[h], CHUNKS[h])]

    kinds = {
        "y": (y_view, z_send, z_recv, yp_send, yp_recv, TOK * 2, 1),
        "p": (p_view, p_send, p_recv, pp_send, pp_recv, 64, 0),
    }

    def partner_message(kind, h, d, s):
        view, _, _, send_sem, recv_sem, height, order = kinds[kind]
        offset = -s if d == 0 else s
        here, there = view(h, offset, k), view(h, offset, 1 - k)
        send, recv = send_sem.at[h, d, s], recv_sem.at[h, d, s]

        def start():
            remote(here, here, send, recv, (partner, col)).start()

        def wait():
            remote(there, there, send, recv, (partner, col)).wait_recv()

        def sent():
            remote(here, here, send, recv, (partner, col)).wait_send()

        cost = CHUNKS[h] * height / PARTNER_RATE
        return Message((kind + "p", h, d, s), {"p": cost}, (order, h), start, wait, None, sent)

    def ring_message(kind, h, d, s):
        view, send_sem, recv_sem, _, _, height, order = kinds[kind]
        step = 1 if d == 0 else -1
        here, there = view(h, -step * (s - 1), k), view(h, -step * s, k)
        send, recv = send_sem.at[h, d, s - 1], recv_sem.at[h, d, s - 1]

        def start():
            remote(here, here, send, recv, z_peer(step)).start()

        def wait():
            remote(there, there, send, recv, z_peer(step)).wait_recv()

        def sent():
            remote(here, here, send, recv, z_peer(step)).wait_send()

        def then():
            if s < 3 or (s == 3 and ring_long(h, d)):
                plan.post(ring_message(kind, h, d, s + 1))
            plan.post(partner_message(kind, h, d, s))

        cost = CHUNKS[h] * height / LINK_RATE
        return Message((kind, h, d, s), {"z+" if d == 0 else "z-": cost}, (order, h, s), start, wait, then, sent)

    def ring_begin(kind, h):
        plan.post(ring_message(kind, h, 0, 1))
        plan.post(ring_message(kind, h, 1, 1))
        plan.post(partner_message(kind, h, 0, 0))

    def ring_names(kind, h):
        names = [(kind + "p", h, 0, 0)]
        for d in (0, 1):
            for s in (1, 2, 3) + ((4,) if ring_long(h, d) else ()):
                names += [(kind, h, d, s), (kind + "p", h, d, s)]
        return names

    def w_view(v, phase, offset, kk):
        first, second = (x, y) if v < 2 else (y, x)
        if phase == 0:
            f, s = (first + offset + 4) % 4, second
        else:
            f, s = slice(None), (second + offset + 4) % 4
        xi, yi = (f, s) if v < 2 else (s, f)
        return wf.at[xi, yi, kk, pl.ds(2 * v, 2)]

    def w_partner(v, phase, j):
        offset = (-1, 1, 2)[j]
        here, there = w_view(v, phase, offset, k), w_view(v, phase, offset, 1 - k)
        send, recv = wp_send.at[v, phase, j], wp_recv.at[v, phase, j]

        def start():
            remote(here, here, send, recv, (partner, col)).start()

        def wait():
            remote(there, there, send, recv, (partner, col)).wait_recv()

        def sent():
            remote(here, here, send, recv, (partner, col)).wait_send()

        cost = 16384 * (4 if phase else 1) / PARTNER_RATE
        return Message(("wp", v, phase, j), {"p": cost}, (0,), start, wait, None, sent)

    def w_message(v, phase, j):
        far = 1 if v % 2 == 0 else -1
        step = (1, -1, far)[j]
        here, there = w_view(v, phase, (0, 0, -far)[j], k), w_view(v, phase, (-1, 1, 2)[j], k)
        send, recv = w_send.at[v, phase, j], w_recv.at[v, phase, j]
        on_x = (v < 2) == (phase == 0)
        link = ("x" if on_x else "y") + ("+" if step > 0 else "-")

        def start():
            remote(here, here, send, recv, along(on_x, step)).start()

        def wait():
            remote(there, there, send, recv, along(on_x, step)).wait_recv()

        def sent():
            remote(here, here, send, recv, along(on_x, step)).wait_send()

        def then():
            if j < 2 and step == far:
                plan.post(w_message(v, phase, 2))
            plan.post(w_partner(v, phase, j))

        cost = 16384 * (4 if phase else 1) / LINK_RATE
        return Message(("w", v, phase, j), {link: cost}, (0, phase), start, wait, then, sent)

    w_names = [(kind, v, phase, j) for kind in ("w", "wp") for v in range(4) for phase in (0, 1) for j in range(3)]

    loads_in[0].wait()
    xt4[x, y] = x_own[...].T
    loads_in[1].wait()
    pl.semaphore_wait(barrier, 30)
    for u in range(len(UNITS)):
        x_begin(u)
    for h in range(len(CHUNKS)):
        ring_begin("y", h)
    plan.poll()

    loads_in[2].wait()
    loads_in[3].wait()

    def own_left(i, carry):
        rows = pl.ds(pl.multiple_of(i * 128, 128), 128)
        parts = jnp.concatenate(split(psi[rows, :], 3), axis=0)
        both = dot(parts, xt4[x, y])
        total = both[0:128] + both[128:256] + both[256:384]
        a_part[pl.ds(pl.multiple_of(i * 8, 8), 8)] = total.reshape(8, 16, TOK)
        return carry

    lax.fori_loop(0, 2, own_left, 0)
    parts = jnp.concatenate(split(om[...], 3), axis=1)
    both = dot(yf[row], parts)
    w_part[...] = (both[:, 0:128] + both[:, 128:256] + both[:, 256:384]).reshape(16, 16, RY)
    plan.now += 4.0

    def loop_row(run):
        def body(j, carry):
            run((row + j) % 16)
            return carry

        lax.fori_loop(1, 16, body, 0)

    def loop_col(run):
        def body(j, carry):
            run((col + j) % 16)
            return carry

        lax.fori_loop(1, 16, body, 0)

    def slot_of(t):
        return 8 * (t % 2) + t // 2

    def rs_left(t):
        return remote(a_part.at[slot_of(t)], a_in.at[me_row], rs_send.at[0, slot_of(t)], rs_recv.at[0, me_row], (t, col))

    def rs_left_in(t):
        here = a_in.at[slot_of(t)]
        return remote(here, here, rs_send.at[0, slot_of(t)], rs_recv.at[0, slot_of(t)], (t, col))

    def rs_right(c):
        return remote(w_part.at[c], w_in.at[col], rs_send.at[1, c], rs_recv.at[1, col], (row, c))

    def rs_right_in(c):
        return remote(w_in.at[c], w_in.at[c], rs_send.at[1, c], rs_recv.at[1, c], (row, c))

    plan.launch(Message(
        ("rs", 1), {link: 1.4 for link in ("x+", "x-", "y+", "y-")}, (0,),
        lambda: loop_col(lambda c: rs_right(c).start()), lambda: loop_col(lambda c: rs_right_in(c).wait_recv()),
        None, lambda: loop_col(lambda c: rs_right(c).wait_send()), 3.5,
    ))
    plan.launch(Message(
        ("rs", 0), {link: 5.6 for link in ("z+", "z-")}, (0,),
        lambda: loop_row(lambda t: rs_left(t).start()), lambda: loop_row(lambda t: rs_left_in(t).wait_recv()),
        None, lambda: loop_row(lambda t: rs_left(t).wait_send()), 3.5,
    ))

    def ga(c):
        return remote(ar.at[col], ar.at[col], ga_send.at[c], ga_recv.at[col], (row, c))

    def ga_in(c):
        return remote(ar.at[c], ar.at[c], ga_send.at[c], ga_recv.at[c], (row, c))

    def gw(t):
        here = wf.at[x, y, k, z]
        return remote(here, here, gw_send.at[t], gw_recv.at[z], (2 * t + k, col))

    def gw_in(t):
        there = wf.at[x, y, k, t]
        return remote(there, there, gw_send.at[t], gw_recv.at[t], (2 * t + k, col))

    def loop_z(run):
        def body(j, carry):
            run((z + j) % 8)
            return carry

        lax.fori_loop(1, 8, body, 0)

    def gc(t):
        return remote(c_all.at[me_row], c_all.at[me_row], gc_send.at[slot_of(t)], gc_recv.at[me_row], (t, col))

    def gc_in(t):
        here = c_all.at[slot_of(t)]
        return remote(here, here, gc_send.at[slot_of(t)], gc_recv.at[slot_of(t)], (t, col))

    last = len(CHUNKS) - 1
    last_cols = pl.ds(CHUNK_AT[last], CHUNKS[last])

    def gp(t):
        here = p_all.at[k, z, :, last_cols]
        return remote(here, here, gp_send.at[slot_of(t)], gp_recv.at[me_row], (t, col))

    def gp_in(t):
        there = p_all.at[t % 2, t // 2, :, last_cols]
        return remote(there, there, gp_send.at[slot_of(t)], gp_recv.at[slot_of(t)], (t, col))

    own_half = wf.at[x, y, k]
    their_half = wf.at[x, y, 1 - k]
    half_out = remote(own_half, own_half, own_send, own_recv, (partner, col))
    half_in = remote(their_half, their_half, own_send, own_recv, (partner, col))

    def reduce_right():
        total = lax.fori_loop(1, 16, lambda j, sum_now: sum_now + w_in[(col + j) % 16], w_part[col])
        wf[x, y, k, z] = total

    def reduce_left():
        total = lax.fori_loop(1, 16, lambda j, sum_now: sum_now + a_in[slot_of((row + j) % 16)], a_part[me_row])
        ar[col] = total

    def send_right():
        plan.launch(Message(
            ("gw",), {"z+": 1.4, "z-": 1.4}, (0,),
            lambda: loop_z(lambda t: gw(t).start()), lambda: loop_z(lambda t: gw_in(t).wait_recv()),
            w_ring, lambda: loop_z(lambda t: gw(t).wait_send()), 3.5,
        ))

    def w_ring():
        for v in range(4):
            for phase in (0,):
                plan.post(w_message(v, phase, 0))
                plan.post(w_message(v, phase, 1))
        plan.post(Message(("wh",), {"p": 0.5}, (0,), half_out.start, half_in.wait_recv, None, half_out.wait_send))

    def send_left():
        plan.launch(Message(
            ("ga",), {link: 2.8 for link in ("x+", "x-", "y+", "y-")}, (0,),
            lambda: loop_col(lambda c: ga(c).start()), lambda: loop_col(lambda c: ga_in(c).wait_recv()),
            None, lambda: loop_col(lambda c: ga(c).wait_send()), 3.5,
        ))

    plan.task("reduce_right", [("rs", 1)], (0,), 0.4, lambda: (reduce_right(), send_right()))
    plan.task("reduce_left", [("rs", 0)], (0,), 0.4, lambda: (reduce_left(), send_left()))
    for v in range(4):
        plan.task(
            ("line", v), [("w", v, 0, j) for j in range(3)], (0,), 0.0,
            lambda v=v: (plan.post(w_message(v, 1, 0)), plan.post(w_message(v, 1, 1))),
        )

    def parts_left():
        for b in range(16):
            ahl[b] = jnp.concatenate(split(ar[b], 3), axis=0)

    def parts_right(quarter):
        def body(i, carry):
            b = quarter * 4 + i
            whl[b] = jnp.concatenate(split(wf[:, :, b % 2, b // 2].reshape(TOK, RY), 3), axis=1)
            return carry

        lax.fori_loop(0, 4, body, 0)

    def left_rows(parts):
        return jnp.concatenate([ahl[b, 0:16 * parts, :] for b in range(16)], axis=1)

    def core_rows():
        both = dot(left_rows(3), whl[...].reshape(16 * TOK, 3 * RY))
        total = both[0:16] + both[16:32] + both[32:48]
        c_all[me_row] = total[:, 0:RY] + total[:, RY:2 * RY] + total[:, 2 * RY:]

    def send_core():
        plan.launch(Message(
            ("gc",), {"z+": 2.8, "z-": 2.8}, (0,),
            lambda: loop_row(lambda t: gc(t).start()), lambda: loop_row(lambda t: gc_in(t).wait_recv()),
            None, lambda: loop_row(lambda t: gc(t).wait_send()), 3.5,
        ))

    plan.task("parts_left", [("ga",)], (1,), 0.3, parts_left)
    needs_w = w_names + [("wh",), ("gw",)]
    for quarter in range(4):
        plan.task(("parts", quarter), needs_w, (0, 1), 0.3, lambda quarter=quarter: parts_right(quarter))
    all_parts = ["parts_left"] + [("parts", quarter) for quarter in range(4)]
    plan.task("core_rows", all_parts, (0, 2), 1.0, lambda: (core_rows(), send_core()))

    def core_t():
        return c_all[...].reshape(RZ, RY).T

    def gram():
        inv_ref[...] = dot(core_t(), c_all[...].reshape(RZ, RY), HIGHEST)

    def pivots(begin):
        lanes = lax.broadcasted_iota(jnp.int32, (RY, RY), 1)
        subs = lax.broadcasted_iota(jnp.int32, (RY, RY), 0)

        def pivot(i, carry):
            now = inv_ref[...]
            line = inv_ref[pl.ds(i, 1), :]
            at_lane = lanes == i
            across = jnp.sum(jnp.where(at_lane, now, 0.0), axis=1, keepdims=True)
            head = jnp.sum(jnp.where(at_lane[0:1], line, 0.0), axis=1, keepdims=True)
            scaled = line / head
            inner = now - across * scaled
            on_line = jnp.where(at_lane, 1.0 / head, scaled)
            off_line = jnp.where(at_lane, -across / head, inner)
            inv_ref[...] = jnp.where(subs == i, on_line, off_line)
            return carry

        lax.fori_loop(begin, begin + 16, pivot, 0)

    def core_map():
        map_ref[...] = dot(inv_ref[...], core_t(), HIGHEST)

    plan.task("gram", [("gc",)], (0, 3), 0.7, gram)
    before = "gram"
    for begin in range(0, RY, 16):
        plan.task(("pivots", begin), [before], (0, 4), 1.1, lambda begin=begin: pivots(begin))
        before = ("pivots", begin)
    plan.task("map", [before], (0, 5), 0.6, core_map)

    def unit_rows(u):
        rows = pl.ds(UNIT_AT[u], UNITS[u])
        return jnp.concatenate([xt4[b // 4, b % 4, rows, :] for b in range(16)], axis=1)

    def right_product(u):
        both = dot(unit_rows(u), whl[:, :, 0:2 * RY].reshape(16 * TOK, 2 * RY))
        q_ref[pl.ds(UNIT_AT[u], UNITS[u]), :] = both[:, 0:RY] + both[:, RY:]

    def chunk(h):
        return yf[:, :, pl.ds(CHUNK_AT[h], CHUNKS[h])].reshape(16 * TOK, CHUNKS[h])

    def g_out(u, h):
        at = (pl.ds(UNIT_AT[u], UNITS[u]), pl.ds(CHUNK_AT[h], CHUNKS[h]))
        return pltpu.make_async_copy(g_acc.at[at], g_hbm.at[at], out_sem.at[u, h])

    def tile(u, h):
        g_acc[pl.ds(UNIT_AT[u], UNITS[u]), pl.ds(CHUNK_AT[h], CHUNKS[h])] = dot(unit_rows(u), chunk(h))

    def tile_out(u, h):
        g_out(u, h).start()
        plan.sent.append(lambda: g_out(u, h).wait())

    def left_product(h):
        both = dot(left_rows(2), chunk(h))
        p_all[k, z, :, pl.ds(CHUNK_AT[h], CHUNKS[h])] = both[0:16] + both[16:32]

    def left_out(h):
        if h < last:
            ring_begin("p", h)
        else:
            plan.launch(Message(
                ("gp",), {"z+": 2.8, "z-": 2.8}, (0,),
                lambda: loop_row(lambda t: gp(t).start()), lambda: loop_row(lambda t: gp_in(t).wait_recv()),
                None, lambda: loop_row(lambda t: gp(t).wait_send()), 3.5,
            ))

    def project(h):
        cols = pl.ds(CHUNK_AT[h], CHUNKS[h])
        r_ref[:, cols] = dot(map_ref[...], p_all[:, :, :, cols].reshape(RZ, CHUNKS[h]), HIGHEST)

    def width(n):
        return (n + 255) // 256

    for u in range(len(UNITS)):
        plan.task(("q", u), x_names(u) + all_parts, (3, u), UNITS[u] * 2.75e-3, lambda u=u: right_product(u))
        for h in range(len(CHUNKS)):
            plan.task(
                ("g", u, h), x_names(u) + ring_names("y", h), (2, max(u, h), u), UNITS[u] * width(CHUNKS[h]) * 2.75e-3,
                lambda u=u, h=h: (tile(u, h), tile_out(u, h)),
            )
    for h in range(len(CHUNKS)):
        plan.task(
            ("pr", h), ring_names("y", h) + ["parts_left"], (1, h), 0.6 * width(CHUNKS[h]),
            lambda h=h: (left_product(h), left_out(h)),
        )
        gathered = ring_names("p", h) if h < last else [("gp",)]
        plan.task(("r", h), gathered + [("pr", h), "map"], (1, 9), 0.3 * width(CHUNKS[h]), lambda h=h: project(h))

    plan.run(LOG)
    p_out = pltpu.make_async_copy(p_all, p_hbm, local_sem.at[0])
    p_out.start()
    for sent in plan.sent:
        sent()
    p_out.wait()


LOG = None


def exchange(inputs, out_grads, om, psi):
    dma = pltpu.SemaphoreType.DMA
    n_u, n_h = len(UNITS), len(CHUNKS)
    anywhere = pl.BlockSpec(memory_space=pl.ANY)
    local = pl.BlockSpec(memory_space=pltpu.VMEM)
    return pl.pallas_call(
        exchange_kernel,
        name="exchange",
        out_shape=(
            jax.ShapeDtypeStruct((BLOCK, RY), F32),
            jax.ShapeDtypeStruct((RY, BLOCK), F32),
            jax.ShapeDtypeStruct((2, 8, 16, BLOCK), F32),
            jax.ShapeDtypeStruct((BLOCK, BLOCK), F32),
        ),
        in_specs=[anywhere] * 4,
        out_specs=(local, local, anywhere, anywhere),
        scratch_shapes=[
            pltpu.VMEM((4, 4, BLOCK, TOK), BF16),
            pltpu.VMEM((16, TOK, BLOCK), BF16),
            pltpu.VMEM((4, 4, 2, 8, 16, RY), F32),
            pltpu.VMEM((16, 16, TOK), F32),
            pltpu.VMEM((16, 48, TOK), BF16),
            pltpu.VMEM((16, TOK, 3 * RY), BF16),
            pltpu.VMEM((BLOCK, BLOCK), F32),
            pltpu.VMEM((2, 8, 16, BLOCK), F32),
            pltpu.VMEM((16, 16, RY), F32),
            pltpu.VMEM((RY, RZ), F32),
            pltpu.VMEM((TOK, BLOCK), BF16),
            pltpu.VMEM((BLOCK, RY), F32),
            pltpu.VMEM((RZ, BLOCK), F32),
            pltpu.VMEM((16, 16, TOK), F32),
            pltpu.VMEM((16, 16, RY), F32),
            pltpu.VMEM((16, 16, TOK), F32),
            pltpu.VMEM((16, 16, RY), F32),
            pltpu.VMEM((RY, RY), F32),
            dma((2, 16)), dma((2, 16)),
            dma((16,)), dma((16,)),
            dma((8,)), dma((8,)),
            dma((16,)), dma((16,)),
            dma((16,)), dma((16,)),
            dma((n_u, 2, 15)), dma((n_u, 2, 15)),
            dma((4, 2, 3)), dma((4, 2, 3)),
            dma((4, 2, 3)), dma((4, 2, 3)),
            dma((n_h, 2, 4)), dma((n_h, 2, 4)),
            dma((n_h, 2, 5)), dma((n_h, 2, 5)),
            dma((n_h, 2, 4)), dma((n_h, 2, 4)),
            dma((n_h, 2, 5)), dma((n_h, 2, 5)),
            dma, dma, dma((4,)), dma((n_u, n_h)),
        ],
        compiler_params=pltpu.CompilerParams(
            collective_id=0, has_side_effects=True, vmem_limit_bytes=62 * 1024 * 1024
        ),
    )(inputs, out_grads, om, psi)


def finish_kernel(g_ref, q_ref, r_ref, p_ref, res_ref, qo_ref, po_ref):
    q_high, q_low = split(q_ref[...], 2)
    r_high, r_low = split(r_ref[...], 2)
    left = jnp.concatenate([q_high, q_low, q_high], axis=1)
    right = jnp.concatenate([r_high, r_high, r_low], axis=0)
    res_ref[...] = g_ref[...] - dot(left, right)
    po_ref[...] = p_ref[...]

    @pl.when(pl.program_id(0) == 0)
    def _():
        qo_ref[...] = q_ref[...]


def finish(g, q, r, p):
    def cols(height):
        return pl.BlockSpec((height, FINISH_COLS), lambda i: (0, i))

    whole = pl.BlockSpec((BLOCK, RY), lambda i: (0, 0))
    return pl.pallas_call(
        finish_kernel,
        name="finish",
        grid=(BLOCK // FINISH_COLS,),
        out_shape=(
            jax.ShapeDtypeStruct((BLOCK, BLOCK), F32),
            jax.ShapeDtypeStruct((BLOCK, RY), F32),
            jax.ShapeDtypeStruct((RZ, BLOCK), F32),
        ),
        in_specs=[cols(BLOCK), whole, cols(RY), cols(RZ)],
        out_specs=(cols(BLOCK), whole, cols(RZ)),
    )(g, q, r, p)


def per_device(inputs, out_grads, range_test, corange_test):
    q, r, p, g = exchange(inputs, out_grads, range_test, corange_test)
    residual, q, p = finish(g, q, r, p.reshape(RZ, BLOCK))
    return (q, p, residual)


def solution(mesh):
    placed = (P("col", "row"), P("row", "col"), P("col", None), P(None, "row"))
    return jax.shard_map(
        per_device,
        mesh=mesh,
        in_specs=placed,
        out_specs=(P("row", None), P(None, "col"), P("row", "col")),
        check_vma=False,
    )
```

```python
import heapq

import jax
import jax.numpy as jnp
from jax import lax
from jax.experimental import pallas as pl
from jax.experimental.pallas import tpu as pltpu
from jax.sharding import PartitionSpec as P

F32 = jnp.float32
BF16 = jnp.bfloat16
HIGHEST = lax.Precision.HIGHEST
MESH = pl.DeviceIdType.MESH

BLOCK = 1152
TOK = 256
RY = 128
RZ = 256
UNITS = (384, 384, 256, 128)
CHUNKS = (512, 512, 128)
FINISH_COLS = 384
EXCHANGE_LIMIT, FINISH_LIMIT = 42, 18

LINK_RATE = 46500.0
PARTNER_RATE = 150000.0
HOP = 1.6
SLACK = 2.5


def starts(sizes):
    return [sum(sizes[:i]) for i in range(len(sizes))]


UNIT_AT = starts(UNITS)
CHUNK_AT = starts(CHUNKS)


def dot(left_side, right_side, precision=None):
    return jnp.dot(left_side, right_side, precision=precision, preferred_element_type=F32)


def split(value, parts):
    out = []
    for _ in range(parts):
        piece = value.astype(BF16)
        value = value - piece.astype(F32)
        out.append(piece)
    return out


class Message:
    def __init__(self, name, loads, order, start, wait, then=None, sent=None, latency=HOP):
        self.name, self.loads, self.order = name, loads, order
        self.start, self.wait, self.then, self.sent, self.latency = start, wait, then, sent, latency


class Plan:
    def __init__(self):
        self.now, self.free, self.queues = 0.0, {}, {}
        self.flying, self.count, self.done, self.tasks, self.sent = [], 0, set(), [], []

    def post(self, message):
        self.count += 1
        link = next(iter(message.loads))
        heapq.heappush(self.queues.setdefault(link, []), (message.order, self.count, message))

    def launch(self, message):
        message.start()
        self.now += 0.03
        end = self.now
        for link, cost in message.loads.items():
            self.free[link] = max(self.now, self.free.get(link, 0.0)) + cost
            end = max(end, self.free[link])
        self.count += 1
        heapq.heappush(self.flying, (end + message.latency, self.count, message))
        if message.sent:
            self.sent.append(message.sent)

    def poll(self):
        for link, queue in self.queues.items():
            while queue and self.free.get(link, 0.0) - self.now < SLACK:
                self.launch(heapq.heappop(queue)[2])

    def task(self, name, needs, order, cost, run):
        self.tasks.append((order, len(self.tasks), name, frozenset(needs), cost, run))

    def finish(self, name):
        self.done.add(name)

    def run(self, log=None):
        while True:
            self.poll()
            if self.flying and self.flying[0][0] <= self.now:
                message = heapq.heappop(self.flying)[2]
                message.wait()
                if log is not None:
                    log.append((round(self.now, 1), "recv", message.name))
                self.now += 0.03
                self.finish(message.name)
                if message.then:
                    message.then()
                continue
            ready = [task for task in self.tasks if task[3] <= self.done]
            if ready:
                best = min(ready)
                self.tasks.remove(best)
                if log is not None:
                    log.append((round(self.now, 1), "task", best[2]))
                best[5]()
                self.now += best[4]
                self.finish(best[2])
                continue
            if not self.flying:
                break
            self.now = self.flying[0][0]
        assert not self.tasks, [(task[2], task[3] - self.done) for task in self.tasks]


def exchange_kernel(
    x_hbm, y_hbm, om_hbm, psi_hbm,
    q_ref, r_ref, p_hbm, g_hbm,
    xt4, yf, wf, ar, ahl, whl, g_acc, p_all, c_all, map_ref,
    x_own, om, psi, a_part, w_part, a_in, w_in, inv_ref,
    rs_send, rs_recv, ga_send, ga_recv, gw_send, gw_recv, gc_send, gc_recv, gp_send, gp_recv,
    x_send, x_recv, w_send, w_recv, wp_send, wp_recv,
    z_send, z_recv, yp_send, yp_recv, p_send, p_recv, pp_send, pp_recv,
    own_send, own_recv, local_sem, out_sem,
):
    row, col = lax.axis_index("row"), lax.axis_index("col")
    z, k = row // 2, row % 2
    x, y = col // 4, col % 4
    partner = row + 1 - 2 * k
    me_row = 8 * k + z

    loads_in = [
        pltpu.make_async_copy(x_hbm, x_own, local_sem.at[0]),
        pltpu.make_async_copy(y_hbm, yf.at[row], local_sem.at[1]),
        pltpu.make_async_copy(psi_hbm, psi, local_sem.at[2]),
        pltpu.make_async_copy(om_hbm, om, local_sem.at[3]),
    ]
    for copy in loads_in:
        copy.start()

    barrier = pltpu.get_barrier_semaphore()

    def greet(j, carry):
        pl.semaphore_signal(barrier, inc=1, device_id=((row + j) % 16, col), device_id_type=MESH)
        pl.semaphore_signal(barrier, inc=1, device_id=(row, (col + j) % 16), device_id_type=MESH)
        return carry

    lax.fori_loop(1, 16, greet, 0)

    def remote(source, target, send, recv, device):
        return pltpu.make_async_remote_copy(
            src_ref=source, dst_ref=target, send_sem=send, recv_sem=recv,
            device_id=device, device_id_type=MESH,
        )

    plan = Plan()

    def along(first_axis, step):
        if first_axis:
            return (row, ((x + step + 4) % 4) * 4 + y)
        return (row, x * 4 + (y + step + 4) % 4)

    def x_view(u, a, o1, o2):
        n = UNITS[u] // 2
        rows = pl.ds(UNIT_AT[u] + n * a, n)
        ox, oy = (o1, o2) if a == 0 else (o2, o1)
        return xt4.at[(x + ox + 4) % 4, (y + oy + 4) % 4, rows, :]

    def x_message(u, a, phase, o1, step, hop):
        on_x = (a == 0) == (phase == 0)
        link = ("x" if on_x else "y") + ("+" if step > 0 else "-")
        if phase == 0:
            slot = {(1, 1): 0, (-1, 1): 1}.get((step, hop), 2)
            out_o, in_o = (-step * (hop - 1), 0), (-step * hop, 0)
        else:
            slot = 3 + 3 * (o1 % 4) + {(1, 1): 0, (-1, 1): 1}.get((step, hop), 2)
            out_o, in_o = (o1, -step * (hop - 1)), (o1, -step * hop)
        here, there = x_view(u, a, *out_o), x_view(u, a, *in_o)
        send, recv = x_send.at[u, a, slot], x_recv.at[u, a, slot]
        name = ("x", u, a, slot)

        def start():
            remote(here, here, send, recv, along(on_x, step)).start()

        def wait():
            remote(there, there, send, recv, along(on_x, step)).wait_recv()

        def sent():
            remote(here, here, send, recv, along(on_x, step)).wait_send()

        def then():
            if phase == 0:
                far = 1 if (u + a) % 2 == 0 else -1
                if hop == 1 and step == far:
                    plan.post(x_message(u, a, 0, 0, step, 2))
                came = (-step * hop) % 4
                plan.post(x_message(u, a, 1, came, 1, 1))
                plan.post(x_message(u, a, 1, came, -1, 1))
            else:
                far = 1 if (o1 % 4 in (0, 2)) == ((u + a) % 2 == 0) else -1
                if hop == 1 and step == far:
                    plan.post(x_message(u, a, 1, o1, step, 2))

        cost = UNITS[u] // 2 * TOK * 2 / LINK_RATE
        return Message(name, {link: cost}, (1, u, phase), start, wait, then, sent)

    def x_names(u):
        return [("x", u, a, slot) for a in (0, 1) for slot in range(15)]

    def x_begin(u):
        for a in (0, 1):
            for phase in (0, 1):
                for step in (1, -1):
                    plan.post(x_message(u, a, phase, 0, step, 1))

    def ring_long(h, d):
        return (h % 2) == d

    def z_peer(step):
        return (2 * ((z + step + 8) % 8) + k, col)

    def y_view(h, offset, kk):
        return yf.at[2 * ((z + offset + 8) % 8) + kk, :, pl.ds(CHUNK_AT[h], CHUNKS[h])]

    def p_view(h, offset, kk):
        return p_all.at[kk, (z + offset + 8) % 8, :, pl.ds(CHUNK_AT[h], CHUNKS[h])]

    kinds = {
        "y": (y_view, z_send, z_recv, yp_send, yp_recv, TOK * 2, 1),
        "p": (p_view, p_send, p_recv, pp_send, pp_recv, 64, 0),
    }

    def partner_message(kind, h, d, s):
        view, _, _, send_sem, recv_sem, height, order = kinds[kind]
        offset = -s if d == 0 else s
        here, there = view(h, offset, k), view(h, offset, 1 - k)
        send, recv = send_sem.at[h, d, s], recv_sem.at[h, d, s]

        def start():
            remote(here, here, send, recv, (partner, col)).start()

        def wait():
            remote(there, there, send, recv, (partner, col)).wait_recv()

        def sent():
            remote(here, here, send, recv, (partner, col)).wait_send()

        cost = CHUNKS[h] * height / PARTNER_RATE
        return Message((kind + "p", h, d, s), {"p": cost}, (order, h), start, wait, None, sent)

    def ring_message(kind, h, d, s):
        view, send_sem, recv_sem, _, _, height, order = kinds[kind]
        step = 1 if d == 0 else -1
        here, there = view(h, -step * (s - 1), k), view(h, -step * s, k)
        send, recv = send_sem.at[h, d, s - 1], recv_sem.at[h, d, s - 1]

        def start():
            remote(here, here, send, recv, z_peer(step)).start()

        def wait():
            remote(there, there, send, recv, z_peer(step)).wait_recv()

        def sent():
            remote(here, here, send, recv, z_peer(step)).wait_send()

        def then():
            if s < 3 or (s == 3 and ring_long(h, d)):
                plan.post(ring_message(kind, h, d, s + 1))
            plan.post(partner_message(kind, h, d, s))

        cost = CHUNKS[h] * height / LINK_RATE
        return Message((kind, h, d, s), {"z+" if d == 0 else "z-": cost}, (order, h, s), start, wait, then, sent)

    def ring_begin(kind, h):
        plan.post(ring_message(kind, h, 0, 1))
        plan.post(ring_message(kind, h, 1, 1))
        plan.post(partner_message(kind, h, 0, 0))

    def ring_names(kind, h):
        names = [(kind + "p", h, 0, 0)]
        for d in (0, 1):
            for s in (1, 2, 3) + ((4,) if ring_long(h, d) else ()):
                names += [(kind, h, d, s), (kind + "p", h, d, s)]
        return names

    def w_view(v, phase, offset, kk):
        first, second = (x, y) if v < 2 else (y, x)
        if phase == 0:
            f, s = (first + offset + 4) % 4, second
        else:
            f, s = slice(None), (second + offset + 4) % 4
        xi, yi = (f, s) if v < 2 else (s, f)
        return wf.at[xi, yi, kk, pl.ds(2 * v, 2)]

    def w_partner(v, phase, j):
        offset = (-1, 1, 2)[j]
        here, there = w_view(v, phase, offset, k), w_view(v, phase, offset, 1 - k)
        send, recv = wp_send.at[v, phase, j], wp_recv.at[v, phase, j]

        def start():
            remote(here, here, send, recv, (partner, col)).start()

        def wait():
            remote(there, there, send, recv, (partner, col)).wait_recv()

        def sent():
            remote(here, here, send, recv, (partner, col)).wait_send()

        cost = 16384 * (4 if phase else 1) / PARTNER_RATE
        return Message(("wp", v, phase, j), {"p": cost}, (0,), start, wait, None, sent)

    def w_message(v, phase, j):
        far = 1 if v % 2 == 0 else -1
        step = (1, -1, far)[j]
        here, there = w_view(v, phase, (0, 0, -far)[j], k), w_view(v, phase, (-1, 1, 2)[j], k)
        send, recv = w_send.at[v, phase, j], w_recv.at[v, phase, j]
        on_x = (v < 2) == (phase == 0)
        link = ("x" if on_x else "y") + ("+" if step > 0 else "-")

        def start():
            remote(here, here, send, recv, along(on_x, step)).start()

        def wait():
            remote(there, there, send, recv, along(on_x, step)).wait_recv()

        def sent():
            remote(here, here, send, recv, along(on_x, step)).wait_send()

        def then():
            if j < 2 and step == far:
                plan.post(w_message(v, phase, 2))
            plan.post(w_partner(v, phase, j))

        cost = 16384 * (4 if phase else 1) / LINK_RATE
        return Message(("w", v, phase, j), {link: cost}, (0, phase), start, wait, then, sent)

    w_names = [(kind, v, phase, j) for kind in ("w", "wp") for v in range(4) for phase in (0, 1) for j in range(3)]

    loads_in[0].wait()
    xt4[x, y] = x_own[...].T
    loads_in[1].wait()
    pl.semaphore_wait(barrier, 30)
    for u in range(len(UNITS)):
        x_begin(u)
    for h in range(len(CHUNKS)):
        ring_begin("y", h)
    plan.poll()

    loads_in[2].wait()
    loads_in[3].wait()

    def own_left(i, carry):
        rows = pl.ds(pl.multiple_of(i * 128, 128), 128)
        parts = jnp.concatenate(split(psi[rows, :], 3), axis=0)
        both = dot(parts, xt4[x, y])
        total = both[0:128] + both[128:256] + both[256:384]
        a_part[pl.ds(pl.multiple_of(i * 8, 8), 8)] = total.reshape(8, 16, TOK)
        return carry

    lax.fori_loop(0, 2, own_left, 0)
    parts = jnp.concatenate(split(om[...], 3), axis=1)
    both = dot(yf[row], parts)
    w_part[...] = (both[:, 0:128] + both[:, 128:256] + both[:, 256:384]).reshape(16, 16, RY)
    plan.now += 4.0

    def loop_row(run):
        def body(j, carry):
            run((row + j) % 16)
            return carry

        lax.fori_loop(1, 16, body, 0)

    def loop_col(run):
        def body(j, carry):
            run((col + j) % 16)
            return carry

        lax.fori_loop(1, 16, body, 0)

    def slot_of(t):
        return 8 * (t % 2) + t // 2

    def rs_left(t):
        return remote(a_part.at[slot_of(t)], a_in.at[me_row], rs_send.at[0, slot_of(t)], rs_recv.at[0, me_row], (t, col))

    def rs_left_in(t):
        here = a_in.at[slot_of(t)]
        return remote(here, here, rs_send.at[0, slot_of(t)], rs_recv.at[0, slot_of(t)], (t, col))

    def rs_right(c):
        return remote(w_part.at[c], w_in.at[col], rs_send.at[1, c], rs_recv.at[1, col], (row, c))

    def rs_right_in(c):
        return remote(w_in.at[c], w_in.at[c], rs_send.at[1, c], rs_recv.at[1, c], (row, c))

    plan.launch(Message(
        ("rs", 1), {link: 1.4 for link in ("x+", "x-", "y+", "y-")}, (0,),
        lambda: loop_col(lambda c: rs_right(c).start()), lambda: loop_col(lambda c: rs_right_in(c).wait_recv()),
        None, lambda: loop_col(lambda c: rs_right(c).wait_send()), 3.5,
    ))
    plan.launch(Message(
        ("rs", 0), {link: 5.6 for link in ("z+", "z-")}, (0,),
        lambda: loop_row(lambda t: rs_left(t).start()), lambda: loop_row(lambda t: rs_left_in(t).wait_recv()),
        None, lambda: loop_row(lambda t: rs_left(t).wait_send()), 3.5,
    ))

    def ga(c):
        return remote(ar.at[col], ar.at[col], ga_send.at[c], ga_recv.at[col], (row, c))

    def ga_in(c):
        return remote(ar.at[c], ar.at[c], ga_send.at[c], ga_recv.at[c], (row, c))

    def gw(t):
        here = wf.at[x, y, k, z]
        return remote(here, here, gw_send.at[t], gw_recv.at[z], (2 * t + k, col))

    def gw_in(t):
        there = wf.at[x, y, k, t]
        return remote(there, there, gw_send.at[t], gw_recv.at[t], (2 * t + k, col))

    def loop_z(run):
        def body(j, carry):
            run((z + j) % 8)
            return carry

        lax.fori_loop(1, 8, body, 0)

    def gc(t):
        return remote(c_all.at[me_row], c_all.at[me_row], gc_send.at[slot_of(t)], gc_recv.at[me_row], (t, col))

    def gc_in(t):
        here = c_all.at[slot_of(t)]
        return remote(here, here, gc_send.at[slot_of(t)], gc_recv.at[slot_of(t)], (t, col))

    last = len(CHUNKS) - 1
    last_cols = pl.ds(CHUNK_AT[last], CHUNKS[last])

    def gp(t):
        here = p_all.at[k, z, :, last_cols]
        return remote(here, here, gp_send.at[slot_of(t)], gp_recv.at[me_row], (t, col))

    def gp_in(t):
        there = p_all.at[t % 2, t // 2, :, last_cols]
        return remote(there, there, gp_send.at[slot_of(t)], gp_recv.at[slot_of(t)], (t, col))

    own_half = wf.at[x, y, k]
    their_half = wf.at[x, y, 1 - k]
    half_out = remote(own_half, own_half, own_send, own_recv, (partner, col))
    half_in = remote(their_half, their_half, own_send, own_recv, (partner, col))

    def reduce_right():
        total = lax.fori_loop(1, 16, lambda j, sum_now: sum_now + w_in[(col + j) % 16], w_part[col])
        wf[x, y, k, z] = total

    def reduce_left():
        total = lax.fori_loop(1, 16, lambda j, sum_now: sum_now + a_in[slot_of((row + j) % 16)], a_part[me_row])
        ar[col] = total

    def send_right():
        plan.launch(Message(
            ("gw",), {"z+": 1.4, "z-": 1.4}, (0,),
            lambda: loop_z(lambda t: gw(t).start()), lambda: loop_z(lambda t: gw_in(t).wait_recv()),
            w_ring, lambda: loop_z(lambda t: gw(t).wait_send()), 3.5,
        ))

    def w_ring():
        for v in range(4):
            for phase in (0,):
                plan.post(w_message(v, phase, 0))
                plan.post(w_message(v, phase, 1))
        plan.post(Message(("wh",), {"p": 0.5}, (0,), half_out.start, half_in.wait_recv, None, half_out.wait_send))

    def send_left():
        plan.launch(Message(
            ("ga",), {link: 2.8 for link in ("x+", "x-", "y+", "y-")}, (0,),
            lambda: loop_col(lambda c: ga(c).start()), lambda: loop_col(lambda c: ga_in(c).wait_recv()),
            None, lambda: loop_col(lambda c: ga(c).wait_send()), 3.5,
        ))

    plan.task("reduce_right", [("rs", 1)], (0,), 0.4, lambda: (reduce_right(), send_right()))
    plan.task("reduce_left", [("rs", 0)], (0,), 0.4, lambda: (reduce_left(), send_left()))
    for v in range(4):
        plan.task(
            ("line", v), [("w", v, 0, j) for j in range(3)], (0,), 0.0,
            lambda v=v: (plan.post(w_message(v, 1, 0)), plan.post(w_message(v, 1, 1))),
        )

    def parts_left():
        for b in range(16):
            ahl[b] = jnp.concatenate(split(ar[b], 3), axis=0)

    def parts_right(quarter):
        def body(i, carry):
            b = quarter * 4 + i
            whl[b] = jnp.concatenate(split(wf[:, :, b % 2, b // 2].reshape(TOK, RY), 3), axis=1)
            return carry

        lax.fori_loop(0, 4, body, 0)

    def left_rows(parts):
        return jnp.concatenate([ahl[b, 0:16 * parts, :] for b in range(16)], axis=1)

    def core_rows():
        both = dot(left_rows(3), whl[...].reshape(16 * TOK, 3 * RY))
        total = both[0:16] + both[16:32] + both[32:48]
        c_all[me_row] = total[:, 0:RY] + total[:, RY:2 * RY] + total[:, 2 * RY:]

    def send_core():
        plan.launch(Message(
            ("gc",), {"z+": 2.8, "z-": 2.8}, (0,),
            lambda: loop_row(lambda t: gc(t).start()), lambda: loop_row(lambda t: gc_in(t).wait_recv()),
            None, lambda: loop_row(lambda t: gc(t).wait_send()), 3.5,
        ))

    plan.task("parts_left", [("ga",)], (1,), 0.3, parts_left)
    needs_w = w_names + [("wh",), ("gw",)]
    for quarter in range(4):
        plan.task(("parts", quarter), needs_w, (0, 1), 0.3, lambda quarter=quarter: parts_right(quarter))
    all_parts = ["parts_left"] + [("parts", quarter) for quarter in range(4)]
    plan.task("core_rows", all_parts, (0, 2), 1.0, lambda: (core_rows(), send_core()))

    def core_t():
        return c_all[...].reshape(RZ, RY).T

    def gram():
        inv_ref[...] = dot(core_t(), c_all[...].reshape(RZ, RY), HIGHEST)

    def pivots(begin):
        lanes = lax.broadcasted_iota(jnp.int32, (RY, RY), 1)
        subs = lax.broadcasted_iota(jnp.int32, (RY, RY), 0)

        def pivot(step, carry):
            i = 2 * step
            now = inv_ref[...]
            line_a = inv_ref[pl.ds(i, 1), :]
            line_b = inv_ref[pl.ds(i + 1, 1), :]
            at_a, at_b = lanes == i, lanes == i + 1
            on_a, on_b = subs == i, subs == i + 1

            def pick(mask, value):
                return jnp.sum(jnp.where(mask, value, 0.0), axis=1, keepdims=True)

            over_a, over_b = pick(at_a, now), pick(at_b, now)
            aa, ab = pick(at_a[0:1], line_a), pick(at_b[0:1], line_a)
            ba, bb = pick(at_a[0:1], line_b), pick(at_b[0:1], line_b)
            head = 1.0 / aa
            ratio_a, ratio_b = ba * head, ab * head
            rest = 1.0 / (bb - ba * ratio_b)
            low, high = -ratio_a * rest, -ratio_b * rest
            top = head + ratio_b * rest * ratio_a
            row_a = top * line_a + high * line_b
            row_b = low * line_a + rest * line_b
            col_a = over_a * top + over_b * low
            col_b = over_a * high + over_b * rest
            inner = now - over_a * row_a - over_b * row_b
            inner = jnp.where(at_a, -col_a, jnp.where(at_b, -col_b, inner))
            row_a = jnp.where(at_a[0:1], top, jnp.where(at_b[0:1], high, row_a))
            row_b = jnp.where(at_a[0:1], low, jnp.where(at_b[0:1], rest, row_b))
            inv_ref[...] = jnp.where(on_a, row_a, jnp.where(on_b, row_b, inner))
            return carry

        lax.fori_loop(begin // 2, begin // 2 + 8, pivot, 0)

    def core_map():
        map_ref[...] = dot(inv_ref[...], core_t(), HIGHEST)

    plan.task("gram", [("gc",)], (0, 3), 0.7, gram)
    before = "gram"
    for begin in range(0, RY, 16):
        plan.task(("pivots", begin), [before], (0, 4), 0.7, lambda begin=begin: pivots(begin))
        before = ("pivots", begin)
    plan.task("map", [before], (0, 5), 0.6, core_map)

    def unit_rows(u):
        rows = pl.ds(UNIT_AT[u], UNITS[u])
        return jnp.concatenate([xt4[b // 4, b % 4, rows, :] for b in range(16)], axis=1)

    def right_product(u):
        both = dot(unit_rows(u), whl[:, :, 0:2 * RY].reshape(16 * TOK, 2 * RY))
        q_ref[pl.ds(UNIT_AT[u], UNITS[u]), :] = both[:, 0:RY] + both[:, RY:]

    def chunk(h):
        return yf[:, :, pl.ds(CHUNK_AT[h], CHUNKS[h])].reshape(16 * TOK, CHUNKS[h])

    def g_out(u, h):
        at = (pl.ds(UNIT_AT[u], UNITS[u]), pl.ds(CHUNK_AT[h], CHUNKS[h]))
        return pltpu.make_async_copy(g_acc.at[at], g_hbm.at[at], out_sem.at[u, h])

    def tile(u, h):
        g_acc[pl.ds(UNIT_AT[u], UNITS[u]), pl.ds(CHUNK_AT[h], CHUNKS[h])] = dot(unit_rows(u), chunk(h))

    def first_tile(h):
        cols = pl.ds(CHUNK_AT[h], CHUNKS[h])
        both = dot(jnp.concatenate([unit_rows(0), left_rows(2)], axis=0), chunk(h))
        g_acc[pl.ds(0, UNITS[0]), cols] = both[0:UNITS[0]]
        p_all[k, z, :, cols] = both[UNITS[0]:UNITS[0] + 16] + both[UNITS[0] + 16:]

    def tile_out(u, h):
        g_out(u, h).start()
        plan.sent.append(lambda: g_out(u, h).wait())

    def left_out(h):
        if h < last:
            ring_begin("p", h)
        else:
            plan.launch(Message(
                ("gp",), {"z+": 2.8, "z-": 2.8}, (0,),
                lambda: loop_row(lambda t: gp(t).start()), lambda: loop_row(lambda t: gp_in(t).wait_recv()),
                None, lambda: loop_row(lambda t: gp(t).wait_send()), 3.5,
            ))

    def project(h):
        cols = pl.ds(CHUNK_AT[h], CHUNKS[h])
        r_ref[:, cols] = dot(map_ref[...], p_all[:, :, :, cols].reshape(RZ, CHUNKS[h]), HIGHEST)

    def width(n):
        return (n + 255) // 256

    for u in range(len(UNITS)):
        plan.task(("q", u), x_names(u) + all_parts, (3, u), UNITS[u] * 2.75e-3, lambda u=u: right_product(u))
        for h in range(len(CHUNKS)) if u else ():
            plan.task(
                ("g", u, h), x_names(u) + ring_names("y", h), (2, max(u, h), u), UNITS[u] * width(CHUNKS[h]) * 2.75e-3,
                lambda u=u, h=h: (tile(u, h), tile_out(u, h)),
            )
    for h in range(len(CHUNKS)):
        plan.task(
            ("pr", h), x_names(0) + ring_names("y", h) + ["parts_left"], (1, h),
            (UNITS[0] + 32) * width(CHUNKS[h]) * 2.75e-3,
            lambda h=h: (first_tile(h), left_out(h), tile_out(0, h)),
        )
        gathered = ring_names("p", h) if h < last else [("gp",)]
        plan.task(("r", h), gathered + [("pr", h), "map"], (1, 9), 0.3 * width(CHUNKS[h]), lambda h=h: project(h))

    plan.run(LOG)
    p_out = pltpu.make_async_copy(p_all, p_hbm, local_sem.at[0])
    p_out.start()
    for sent in plan.sent:
        sent()
    p_out.wait()


LOG = None


def exchange(inputs, out_grads, om, psi):
    dma = pltpu.SemaphoreType.DMA
    n_u, n_h = len(UNITS), len(CHUNKS)
    anywhere = pl.BlockSpec(memory_space=pl.ANY)
    local = pl.BlockSpec(memory_space=pltpu.VMEM)
    return pl.pallas_call(
        exchange_kernel,
        name="exchange",
        out_shape=(
            jax.ShapeDtypeStruct((BLOCK, RY), F32),
            jax.ShapeDtypeStruct((RY, BLOCK), F32),
            jax.ShapeDtypeStruct((2, 8, 16, BLOCK), F32),
            jax.ShapeDtypeStruct((BLOCK, BLOCK), F32),
        ),
        in_specs=[pl.BlockSpec(memory_space=pltpu.HBM)] * 4,
        out_specs=(local, local, anywhere, anywhere),
        scratch_shapes=[
            pltpu.VMEM((4, 4, BLOCK, TOK), BF16),
            pltpu.VMEM((16, TOK, BLOCK), BF16),
            pltpu.VMEM((4, 4, 2, 8, 16, RY), F32),
            pltpu.VMEM((16, 16, TOK), F32),
            pltpu.VMEM((16, 48, TOK), BF16),
            pltpu.VMEM((16, TOK, 3 * RY), BF16),
            pltpu.VMEM((BLOCK, BLOCK), F32),
            pltpu.VMEM((2, 8, 16, BLOCK), F32),
            pltpu.VMEM((16, 16, RY), F32),
            pltpu.VMEM((RY, RZ), F32),
            pltpu.VMEM((TOK, BLOCK), BF16),
            pltpu.VMEM((BLOCK, RY), F32),
            pltpu.VMEM((RZ, BLOCK), F32),
            pltpu.VMEM((16, 16, TOK), F32),
            pltpu.VMEM((16, 16, RY), F32),
            pltpu.VMEM((16, 16, TOK), F32),
            pltpu.VMEM((16, 16, RY), F32),
            pltpu.VMEM((RY, RY), F32),
            dma((2, 16)), dma((2, 16)),
            dma((16,)), dma((16,)),
            dma((8,)), dma((8,)),
            dma((16,)), dma((16,)),
            dma((16,)), dma((16,)),
            dma((n_u, 2, 15)), dma((n_u, 2, 15)),
            dma((4, 2, 3)), dma((4, 2, 3)),
            dma((4, 2, 3)), dma((4, 2, 3)),
            dma((n_h, 2, 4)), dma((n_h, 2, 4)),
            dma((n_h, 2, 5)), dma((n_h, 2, 5)),
            dma((n_h, 2, 4)), dma((n_h, 2, 4)),
            dma((n_h, 2, 5)), dma((n_h, 2, 5)),
            dma, dma, dma((4,)), dma((n_u, n_h)),
        ],
        compiler_params=pltpu.CompilerParams(
            collective_id=0, has_side_effects=True, vmem_limit_bytes=EXCHANGE_LIMIT * 1024 * 1024
        ),
    )(inputs, out_grads, om, psi)


def finish_kernel(g_ref, q_ref, r_ref, p_ref, res_ref, qo_ref, po_ref):
    q_high, q_low = split(q_ref[...], 2)
    r_high, r_low = split(r_ref[...], 2)
    left = jnp.concatenate([q_high, q_low, q_high], axis=1)
    right = jnp.concatenate([r_high, r_high, r_low], axis=0)
    res_ref[...] = g_ref[...] - dot(left, right)
    po_ref[...] = p_ref[...]

    @pl.when(pl.program_id(0) == 0)
    def _():
        qo_ref[...] = q_ref[...]


def finish(g, q, r, p):
    def cols(height):
        return pl.BlockSpec((height, FINISH_COLS), lambda i: (0, i))

    whole = pl.BlockSpec((BLOCK, RY), lambda i: (0, 0))
    return pl.pallas_call(
        finish_kernel,
        name="finish",
        grid=(BLOCK // FINISH_COLS,),
        out_shape=(
            jax.ShapeDtypeStruct((BLOCK, BLOCK), F32),
            jax.ShapeDtypeStruct((BLOCK, RY), F32),
            jax.ShapeDtypeStruct((RZ, BLOCK), F32),
        ),
        in_specs=[cols(BLOCK), whole, cols(RY), cols(RZ)],
        out_specs=(cols(BLOCK), whole, cols(RZ)),
        compiler_params=pltpu.CompilerParams(vmem_limit_bytes=FINISH_LIMIT * 1024 * 1024),
    )(g, q, r, p)


def per_device(inputs, out_grads, range_test, corange_test):
    q, r, p, g = exchange(inputs, out_grads, range_test, corange_test)
    residual, q, p = finish(g, q, r, p.reshape(RZ, BLOCK))
    return (q, p, residual)


def solution(mesh):
    placed = (P("col", "row"), P("row", "col"), P("col", None), P(None, "row"))
    return jax.shard_map(
        per_device,
        mesh=mesh,
        in_specs=placed,
        out_specs=(P("row", None), P(None, "col"), P("row", "col")),
        check_vma=False,
    )
```

```python
import heapq

import jax
import jax.numpy as jnp
from jax import lax
from jax.experimental import pallas as pl
from jax.experimental.pallas import tpu as pltpu
from jax.sharding import PartitionSpec as P

F32 = jnp.float32
BF16 = jnp.bfloat16
HIGHEST = lax.Precision.HIGHEST
MESH = pl.DeviceIdType.MESH

BLOCK = 1152
TOK = 256
RY = 128
RZ = 256
UNITS = (384, 384, 256, 128)
CHUNKS = (512, 512, 128)
FINISH_COLS = 384
EXCHANGE_LIMIT, FINISH_LIMIT = 42, 18

LINK_RATE = 46500.0
PARTNER_RATE = 150000.0
HOP = 1.6
SLACK = 2.5


def starts(sizes):
    return [sum(sizes[:i]) for i in range(len(sizes))]


UNIT_AT = starts(UNITS)
CHUNK_AT = starts(CHUNKS)


def dot(left_side, right_side, precision=None):
    return jnp.dot(left_side, right_side, precision=precision, preferred_element_type=F32)


def split(value, parts):
    out = []
    for _ in range(parts):
        piece = value.astype(BF16)
        value = value - piece.astype(F32)
        out.append(piece)
    return out


class Message:
    def __init__(self, name, loads, order, start, wait, then=None, sent=None, latency=HOP):
        self.name, self.loads, self.order = name, loads, order
        self.start, self.wait, self.then, self.sent, self.latency = start, wait, then, sent, latency


class Plan:
    def __init__(self):
        self.now, self.free, self.queues = 0.0, {}, {}
        self.flying, self.count, self.done, self.tasks, self.sent = [], 0, set(), [], []

    def post(self, message):
        self.count += 1
        link = next(iter(message.loads))
        heapq.heappush(self.queues.setdefault(link, []), (message.order, self.count, message))

    def launch(self, message):
        message.start()
        self.now += 0.03
        end = self.now
        for link, cost in message.loads.items():
            self.free[link] = max(self.now, self.free.get(link, 0.0)) + cost
            end = max(end, self.free[link])
        self.count += 1
        heapq.heappush(self.flying, (end + message.latency, self.count, message))
        if message.sent:
            self.sent.append(message.sent)

    def poll(self):
        for link, queue in self.queues.items():
            while queue and self.free.get(link, 0.0) - self.now < SLACK:
                self.launch(heapq.heappop(queue)[2])

    def task(self, name, needs, order, cost, run):
        self.tasks.append((order, len(self.tasks), name, frozenset(needs), cost, run))

    def finish(self, name):
        self.done.add(name)

    def run(self, log=None):
        while True:
            self.poll()
            if self.flying and self.flying[0][0] <= self.now:
                message = heapq.heappop(self.flying)[2]
                message.wait()
                if log is not None:
                    log.append((round(self.now, 1), "recv", message.name))
                self.now += 0.03
                self.finish(message.name)
                if message.then:
                    message.then()
                continue
            ready = [task for task in self.tasks if task[3] <= self.done]
            if ready:
                best = min(ready)
                self.tasks.remove(best)
                if log is not None:
                    log.append((round(self.now, 1), "task", best[2]))
                best[5]()
                self.now += best[4]
                self.finish(best[2])
                continue
            if not self.flying:
                break
            self.now = self.flying[0][0]
        assert not self.tasks, [(task[2], task[3] - self.done) for task in self.tasks]


def exchange_kernel(
    x_hbm, y_hbm, om_hbm, psi_hbm,
    q_ref, r_ref, p_hbm, g_hbm,
    xt4, yf, wf, ar, ahl, whl, g_acc, p_all, c_all, map_ref,
    x_own, om, psi, a_part, w_part, a_pre, a_in, w_in, inv_ref,
    rs_send, rs_recv, ga_send, ga_recv, gw_send, gw_recv, gc_send, gc_recv, gp_send, gp_recv,
    x_send, x_recv, w_send, w_recv, wp_send, wp_recv,
    z_send, z_recv, yp_send, yp_recv, p_send, p_recv, pp_send, pp_recv,
    own_send, own_recv, local_sem, out_sem,
):
    row, col = lax.axis_index("row"), lax.axis_index("col")
    z, k = row // 2, row % 2
    x, y = col // 4, col % 4
    partner = row + 1 - 2 * k
    me_row = 8 * k + z

    loads_in = [
        pltpu.make_async_copy(x_hbm, x_own, local_sem.at[0]),
        pltpu.make_async_copy(y_hbm, yf.at[row], local_sem.at[1]),
        pltpu.make_async_copy(psi_hbm, psi, local_sem.at[2]),
        pltpu.make_async_copy(om_hbm, om, local_sem.at[3]),
    ]
    for copy in loads_in:
        copy.start()

    barrier = pltpu.get_barrier_semaphore()

    def greet(j, carry):
        pl.semaphore_signal(barrier, inc=1, device_id=((row + j) % 16, col), device_id_type=MESH)
        pl.semaphore_signal(barrier, inc=1, device_id=(row, (col + j) % 16), device_id_type=MESH)
        return carry

    lax.fori_loop(1, 16, greet, 0)

    def remote(source, target, send, recv, device):
        return pltpu.make_async_remote_copy(
            src_ref=source, dst_ref=target, send_sem=send, recv_sem=recv,
            device_id=device, device_id_type=MESH,
        )

    plan = Plan()

    def along(first_axis, step):
        if first_axis:
            return (row, ((x + step + 4) % 4) * 4 + y)
        return (row, x * 4 + (y + step + 4) % 4)

    def x_view(u, a, o1, o2):
        n = UNITS[u] // 2
        rows = pl.ds(UNIT_AT[u] + n * a, n)
        ox, oy = (o1, o2) if a == 0 else (o2, o1)
        return xt4.at[(x + ox + 4) % 4, (y + oy + 4) % 4, rows, :]

    def x_message(u, a, phase, o1, step, hop):
        on_x = (a == 0) == (phase == 0)
        link = ("x" if on_x else "y") + ("+" if step > 0 else "-")
        if phase == 0:
            slot = {(1, 1): 0, (-1, 1): 1}.get((step, hop), 2)
            out_o, in_o = (-step * (hop - 1), 0), (-step * hop, 0)
        else:
            slot = 3 + 3 * (o1 % 4) + {(1, 1): 0, (-1, 1): 1}.get((step, hop), 2)
            out_o, in_o = (o1, -step * (hop - 1)), (o1, -step * hop)
        here, there = x_view(u, a, *out_o), x_view(u, a, *in_o)
        send, recv = x_send.at[u, a, slot], x_recv.at[u, a, slot]
        name = ("x", u, a, slot)

        def start():
            remote(here, here, send, recv, along(on_x, step)).start()

        def wait():
            remote(there, there, send, recv, along(on_x, step)).wait_recv()

        def sent():
            remote(here, here, send, recv, along(on_x, step)).wait_send()

        def then():
            if phase == 0:
                far = 1 if (u + a) % 2 == 0 else -1
                if hop == 1 and step == far:
                    plan.post(x_message(u, a, 0, 0, step, 2))
                came = (-step * hop) % 4
                plan.post(x_message(u, a, 1, came, 1, 1))
                plan.post(x_message(u, a, 1, came, -1, 1))
            else:
                far = 1 if (o1 % 4 in (0, 2)) == ((u + a) % 2 == 0) else -1
                if hop == 1 and step == far:
                    plan.post(x_message(u, a, 1, o1, step, 2))

        cost = UNITS[u] // 2 * TOK * 2 / LINK_RATE
        return Message(name, {link: cost}, (1, u, phase), start, wait, then, sent)

    def x_names(u):
        return [("x", u, a, slot) for a in (0, 1) for slot in range(15)]

    def x_begin(u):
        for a in (0, 1):
            for phase in (0, 1):
                for step in (1, -1):
                    plan.post(x_message(u, a, phase, 0, step, 1))

    def ring_long(h, d):
        return (h % 2) == d

    def z_peer(step):
        return (2 * ((z + step + 8) % 8) + k, col)

    def y_view(h, offset, kk):
        return yf.at[2 * ((z + offset + 8) % 8) + kk, :, pl.ds(CHUNK_AT[h], CHUNKS[h])]

    def p_view(h, offset, kk):
        return p_all.at[kk, (z + offset + 8) % 8, :, pl.ds(CHUNK_AT[h], CHUNKS[h])]

    kinds = {
        "y": (y_view, z_send, z_recv, yp_send, yp_recv, TOK * 2, 1),
        "p": (p_view, p_send, p_recv, pp_send, pp_recv, 64, 0),
    }

    def partner_message(kind, h, d, s):
        view, _, _, send_sem, recv_sem, height, order = kinds[kind]
        offset = -s if d == 0 else s
        here, there = view(h, offset, k), view(h, offset, 1 - k)
        send, recv = send_sem.at[h, d, s], recv_sem.at[h, d, s]

        def start():
            remote(here, here, send, recv, (partner, col)).start()

        def wait():
            remote(there, there, send, recv, (partner, col)).wait_recv()

        def sent():
            remote(here, here, send, recv, (partner, col)).wait_send()

        cost = CHUNKS[h] * height / PARTNER_RATE
        return Message((kind + "p", h, d, s), {"p": cost}, (order, h), start, wait, None, sent)

    def ring_message(kind, h, d, s):
        view, send_sem, recv_sem, _, _, height, order = kinds[kind]
        step = 1 if d == 0 else -1
        here, there = view(h, -step * (s - 1), k), view(h, -step * s, k)
        send, recv = send_sem.at[h, d, s - 1], recv_sem.at[h, d, s - 1]

        def start():
            remote(here, here, send, recv, z_peer(step)).start()

        def wait():
            remote(there, there, send, recv, z_peer(step)).wait_recv()

        def sent():
            remote(here, here, send, recv, z_peer(step)).wait_send()

        def then():
            if s < 3 or (s == 3 and ring_long(h, d)):
                plan.post(ring_message(kind, h, d, s + 1))
            plan.post(partner_message(kind, h, d, s))

        cost = CHUNKS[h] * height / LINK_RATE
        return Message((kind, h, d, s), {"z+" if d == 0 else "z-": cost}, (order, h, s), start, wait, then, sent)

    def ring_begin(kind, h):
        plan.post(ring_message(kind, h, 0, 1))
        plan.post(ring_message(kind, h, 1, 1))
        plan.post(partner_message(kind, h, 0, 0))

    def ring_names(kind, h):
        names = [(kind + "p", h, 0, 0)]
        for d in (0, 1):
            for s in (1, 2, 3) + ((4,) if ring_long(h, d) else ()):
                names += [(kind, h, d, s), (kind + "p", h, d, s)]
        return names

    def w_view(v, phase, offset, kk):
        first, second = (x, y) if v < 2 else (y, x)
        if phase == 0:
            f, s = (first + offset + 4) % 4, second
        else:
            f, s = slice(None), (second + offset + 4) % 4
        xi, yi = (f, s) if v < 2 else (s, f)
        return wf.at[xi, yi, kk, pl.ds(2 * v, 2)]

    def w_partner(v, phase, j):
        offset = (-1, 1, 2)[j]
        here, there = w_view(v, phase, offset, k), w_view(v, phase, offset, 1 - k)
        send, recv = wp_send.at[v, phase, j], wp_recv.at[v, phase, j]

        def start():
            remote(here, here, send, recv, (partner, col)).start()

        def wait():
            remote(there, there, send, recv, (partner, col)).wait_recv()

        def sent():
            remote(here, here, send, recv, (partner, col)).wait_send()

        cost = 16384 * (4 if phase else 1) / PARTNER_RATE
        return Message(("wp", v, phase, j), {"p": cost}, (0,), start, wait, None, sent)

    def w_message(v, phase, j):
        far = 1 if v % 2 == 0 else -1
        step = (1, -1, far)[j]
        here, there = w_view(v, phase, (0, 0, -far)[j], k), w_view(v, phase, (-1, 1, 2)[j], k)
        send, recv = w_send.at[v, phase, j], w_recv.at[v, phase, j]
        on_x = (v < 2) == (phase == 0)
        link = ("x" if on_x else "y") + ("+" if step > 0 else "-")

        def start():
            remote(here, here, send, recv, along(on_x, step)).start()

        def wait():
            remote(there, there, send, recv, along(on_x, step)).wait_recv()

        def sent():
            remote(here, here, send, recv, along(on_x, step)).wait_send()

        def then():
            if j < 2 and step == far:
                plan.post(w_message(v, phase, 2))
            plan.post(w_partner(v, phase, j))

        cost = 16384 * (4 if phase else 1) / LINK_RATE
        return Message(("w", v, phase, j), {link: cost}, (0, phase), start, wait, then, sent)

    w_names = [(kind, v, phase, j) for kind in ("w", "wp") for v in range(4) for phase in (0, 1) for j in range(3)]

    loads_in[0].wait()
    xt4[x, y] = x_own[...].T
    loads_in[1].wait()
    pl.semaphore_wait(barrier, 30)
    for u in range(len(UNITS)):
        x_begin(u)
    for h in range(len(CHUNKS)):
        ring_begin("y", h)
    plan.poll()

    loads_in[2].wait()
    loads_in[3].wait()

    def own_left(i, carry):
        rows = pl.ds(pl.multiple_of(i * 128, 128), 128)
        parts = jnp.concatenate(split(psi[rows, :], 3), axis=0)
        both = dot(parts, xt4[x, y])
        total = both[0:128] + both[128:256] + both[256:384]
        a_part[pl.ds(pl.multiple_of(i * 8, 8), 8)] = total.reshape(8, 16, TOK)
        return carry

    lax.fori_loop(0, 2, own_left, 0)
    parts = jnp.concatenate(split(om[...], 3), axis=1)
    both = dot(yf[row], parts)
    w_part[...] = (both[:, 0:128] + both[:, 128:256] + both[:, 256:384]).reshape(16, 16, RY)
    plan.now += 4.0

    def loop_row(run):
        def body(j, carry):
            run((row + j) % 16)
            return carry

        lax.fori_loop(1, 16, body, 0)

    def loop_col(run):
        def body(j, carry):
            run((col + j) % 16)
            return carry

        lax.fori_loop(1, 16, body, 0)

    def slot_of(t):
        return 8 * (t % 2) + t // 2

    mine = pl.ds(pl.multiple_of(8 * k, 8), 8)
    theirs = pl.ds(pl.multiple_of(8 * (1 - k), 8), 8)

    def loop_z(run):
        def body(j, carry):
            run((z + j) % 8)
            return carry

        lax.fori_loop(1, 8, body, 0)

    pre_out = remote(a_part.at[theirs], a_pre, rs_send.at[0, 8], rs_recv.at[0, 8], (partner, col))

    def rs_left(t):
        return remote(a_part.at[8 * k + t], a_in.at[z], rs_send.at[0, t], rs_recv.at[0, z], (2 * t + k, col))

    def rs_left_in(t):
        return remote(a_in.at[t], a_in.at[t], rs_send.at[0, t], rs_recv.at[0, t], (2 * t + k, col))

    def rs_right(c):
        return remote(w_part.at[c], w_in.at[col], rs_send.at[1, c], rs_recv.at[1, col], (row, c))

    def rs_right_in(c):
        return remote(w_in.at[c], w_in.at[c], rs_send.at[1, c], rs_recv.at[1, c], (row, c))

    plan.launch(Message(
        ("rs", 1), {link: 1.4 for link in ("x+", "x-", "y+", "y-")}, (0,),
        lambda: loop_col(lambda c: rs_right(c).start()), lambda: loop_col(lambda c: rs_right_in(c).wait_recv()),
        None, lambda: loop_col(lambda c: rs_right(c).wait_send()), 3.5,
    ))
    plan.launch(Message(
        ("pre",), {"p": 0.9}, (0,), pre_out.start, pre_out.wait_recv, None, pre_out.wait_send
    ))

    def scatter_left():
        a_part[mine] = a_part[mine] + a_pre[...]
        plan.launch(Message(
            ("rs", 0), {link: 2.8 for link in ("z+", "z-")}, (0,),
            lambda: loop_z(lambda t: rs_left(t).start()), lambda: loop_z(lambda t: rs_left_in(t).wait_recv()),
            None, lambda: loop_z(lambda t: rs_left(t).wait_send()), 3.5,
        ))

    plan.task("scatter_left", [("pre",)], (0,), 0.3, scatter_left)

    def ga(c):
        return remote(ar.at[col], ar.at[col], ga_send.at[c], ga_recv.at[col], (row, c))

    def ga_in(c):
        return remote(ar.at[c], ar.at[c], ga_send.at[c], ga_recv.at[c], (row, c))

    def gw(t):
        here = wf.at[x, y, k, z]
        return remote(here, here, gw_send.at[t], gw_recv.at[z], (2 * t + k, col))

    def gw_in(t):
        there = wf.at[x, y, k, t]
        return remote(there, there, gw_send.at[t], gw_recv.at[t], (2 * t + k, col))

    def spread(name, cost, piece, whole, send_sem, recv_sem):
        def out(t):
            return remote(piece(z), piece(z), send_sem.at[t], recv_sem.at[z], (2 * t + k, col))

        def into(t):
            return remote(piece(t), piece(t), send_sem.at[t], recv_sem.at[t], (2 * t + k, col))

        half = remote(whole(k), whole(k), send_sem.at[8], recv_sem.at[8], (partner, col))
        other = remote(whole(1 - k), whole(1 - k), send_sem.at[8], recv_sem.at[8], (partner, col))
        plan.launch(Message(
            (name,), {"z+": cost, "z-": cost}, (0,),
            lambda: loop_z(lambda t: out(t).start()), lambda: loop_z(lambda t: into(t).wait_recv()),
            lambda: plan.post(Message(
                (name, 1), {"p": 0.4}, (0,), half.start, other.wait_recv, None, half.wait_send
            )),
            lambda: loop_z(lambda t: out(t).wait_send()), 3.5,
        ))

    last = len(CHUNKS) - 1
    last_cols = pl.ds(CHUNK_AT[last], CHUNKS[last])

    own_half = wf.at[x, y, k]
    their_half = wf.at[x, y, 1 - k]
    half_out = remote(own_half, own_half, own_send, own_recv, (partner, col))
    half_in = remote(their_half, their_half, own_send, own_recv, (partner, col))

    def reduce_right():
        total = lax.fori_loop(1, 16, lambda j, sum_now: sum_now + w_in[(col + j) % 16], w_part[col])
        wf[x, y, k, z] = total

    def reduce_left():
        total = lax.fori_loop(1, 8, lambda j, sum_now: sum_now + a_in[(z + j) % 8], a_part[me_row])
        ar[col] = total

    def send_right():
        plan.launch(Message(
            ("gw",), {"z+": 1.4, "z-": 1.4}, (0,),
            lambda: loop_z(lambda t: gw(t).start()), lambda: loop_z(lambda t: gw_in(t).wait_recv()),
            w_ring, lambda: loop_z(lambda t: gw(t).wait_send()), 3.5,
        ))

    def w_ring():
        for v in range(4):
            for phase in (0,):
                plan.post(w_message(v, phase, 0))
                plan.post(w_message(v, phase, 1))
        plan.post(Message(("wh",), {"p": 0.5}, (0,), half_out.start, half_in.wait_recv, None, half_out.wait_send))

    def send_left():
        plan.launch(Message(
            ("ga",), {link: 2.8 for link in ("x+", "x-", "y+", "y-")}, (0,),
            lambda: loop_col(lambda c: ga(c).start()), lambda: loop_col(lambda c: ga_in(c).wait_recv()),
            None, lambda: loop_col(lambda c: ga(c).wait_send()), 3.5,
        ))

    plan.task("reduce_right", [("rs", 1)], (0,), 0.4, lambda: (reduce_right(), send_right()))
    plan.task("reduce_left", [("rs", 0)], (0,), 0.4, lambda: (reduce_left(), send_left()))
    for v in range(4):
        plan.task(
            ("line", v), [("w", v, 0, j) for j in range(3)], (0,), 0.0,
            lambda v=v: (plan.post(w_message(v, 1, 0)), plan.post(w_message(v, 1, 1))),
        )

    def parts_left():
        for b in range(16):
            ahl[b] = jnp.concatenate(split(ar[b], 3), axis=0)

    def parts_right(quarter):
        def body(i, carry):
            b = quarter * 4 + i
            whl[b] = jnp.concatenate(split(wf[:, :, b % 2, b // 2].reshape(TOK, RY), 3), axis=1)
            return carry

        lax.fori_loop(0, 4, body, 0)

    def left_rows(parts):
        return jnp.concatenate([ahl[b, 0:16 * parts, :] for b in range(16)], axis=1)

    def core_rows():
        both = dot(left_rows(3), whl[...].reshape(16 * TOK, 3 * RY))
        total = both[0:16] + both[16:32] + both[32:48]
        c_all[me_row] = total[:, 0:RY] + total[:, RY:2 * RY] + total[:, 2 * RY:]

    def send_core():
        spread(
            "gc", 1.4, lambda t: c_all.at[8 * k + t],
            lambda kk: c_all.at[pl.ds(pl.multiple_of(8 * kk, 8), 8)], gc_send, gc_recv,
        )

    plan.task("parts_left", [("ga",)], (1,), 0.3, parts_left)
    needs_w = w_names + [("wh",), ("gw",)]
    for quarter in range(4):
        plan.task(("parts", quarter), needs_w, (0, 1), 0.3, lambda quarter=quarter: parts_right(quarter))
    all_parts = ["parts_left"] + [("parts", quarter) for quarter in range(4)]
    plan.task("core_rows", all_parts, (0, 2), 1.0, lambda: (core_rows(), send_core()))

    def core_t():
        return c_all[...].reshape(RZ, RY).T

    def gram():
        inv_ref[...] = dot(core_t(), c_all[...].reshape(RZ, RY), HIGHEST)

    def pivots(begin):
        lanes = lax.broadcasted_iota(jnp.int32, (RY, RY), 1)
        subs = lax.broadcasted_iota(jnp.int32, (RY, RY), 0)

        def pivot(step, carry):
            i = 2 * step
            now = inv_ref[...]
            line_a = inv_ref[pl.ds(i, 1), :]
            line_b = inv_ref[pl.ds(i + 1, 1), :]
            at_a, at_b = lanes == i, lanes == i + 1
            on_a, on_b = subs == i, subs == i + 1

            def pick(mask, value):
                return jnp.sum(jnp.where(mask, value, 0.0), axis=1, keepdims=True)

            over_a, over_b = pick(at_a, now), pick(at_b, now)
            aa, ab = pick(at_a[0:1], line_a), pick(at_b[0:1], line_a)
            ba, bb = pick(at_a[0:1], line_b), pick(at_b[0:1], line_b)
            head = 1.0 / aa
            ratio_a, ratio_b = ba * head, ab * head
            rest = 1.0 / (bb - ba * ratio_b)
            low, high = -ratio_a * rest, -ratio_b * rest
            top = head + ratio_b * rest * ratio_a
            row_a = top * line_a + high * line_b
            row_b = low * line_a + rest * line_b
            col_a = over_a * top + over_b * low
            col_b = over_a * high + over_b * rest
            inner = now - over_a * row_a - over_b * row_b
            inner = jnp.where(at_a, -col_a, jnp.where(at_b, -col_b, inner))
            row_a = jnp.where(at_a[0:1], top, jnp.where(at_b[0:1], high, row_a))
            row_b = jnp.where(at_a[0:1], low, jnp.where(at_b[0:1], rest, row_b))
            inv_ref[...] = jnp.where(on_a, row_a, jnp.where(on_b, row_b, inner))
            return carry

        lax.fori_loop(begin // 2, begin // 2 + 8, pivot, 0)

    def core_map():
        map_ref[...] = dot(inv_ref[...], core_t(), HIGHEST)

    plan.task("gram", [("gc",), ("gc", 1)], (0, 3), 0.7, gram)
    before = "gram"
    for begin in range(0, RY, 16):
        plan.task(("pivots", begin), [before], (0, 4), 0.7, lambda begin=begin: pivots(begin))
        before = ("pivots", begin)
    plan.task("map", [before], (0, 5), 0.6, core_map)

    def unit_rows(u):
        rows = pl.ds(UNIT_AT[u], UNITS[u])
        return jnp.concatenate([xt4[b // 4, b % 4, rows, :] for b in range(16)], axis=1)

    def right_product(u):
        both = dot(unit_rows(u), whl[:, :, 0:2 * RY].reshape(16 * TOK, 2 * RY))
        q_ref[pl.ds(UNIT_AT[u], UNITS[u]), :] = both[:, 0:RY] + both[:, RY:]

    def chunk(h):
        return yf[:, :, pl.ds(CHUNK_AT[h], CHUNKS[h])].reshape(16 * TOK, CHUNKS[h])

    def g_out(u, h):
        at = (pl.ds(UNIT_AT[u], UNITS[u]), pl.ds(CHUNK_AT[h], CHUNKS[h]))
        return pltpu.make_async_copy(g_acc.at[at], g_hbm.at[at], out_sem.at[u, h])

    def tile(u, h):
        g_acc[pl.ds(UNIT_AT[u], UNITS[u]), pl.ds(CHUNK_AT[h], CHUNKS[h])] = dot(unit_rows(u), chunk(h))

    def first_tile(h):
        cols = pl.ds(CHUNK_AT[h], CHUNKS[h])
        both = dot(jnp.concatenate([unit_rows(0), left_rows(2)], axis=0), chunk(h))
        g_acc[pl.ds(0, UNITS[0]), cols] = both[0:UNITS[0]]
        p_all[k, z, :, cols] = both[UNITS[0]:UNITS[0] + 16] + both[UNITS[0] + 16:]

    def tile_out(u, h):
        g_out(u, h).start()
        plan.sent.append(lambda: g_out(u, h).wait())

    def left_out(h):
        if h < last:
            ring_begin("p", h)
        else:
            spread(
                "gp", 1.4, lambda t: p_all.at[k, t, :, last_cols],
                lambda kk: p_all.at[kk, :, :, last_cols], gp_send, gp_recv,
            )

    def project(h):
        cols = pl.ds(CHUNK_AT[h], CHUNKS[h])
        r_ref[:, cols] = dot(map_ref[...], p_all[:, :, :, cols].reshape(RZ, CHUNKS[h]), HIGHEST)

    def width(n):
        return (n + 255) // 256

    for u in range(len(UNITS)):
        plan.task(("q", u), x_names(u) + all_parts, (3, u), UNITS[u] * 2.75e-3, lambda u=u: right_product(u))
        for h in range(len(CHUNKS)) if u else ():
            plan.task(
                ("g", u, h), x_names(u) + ring_names("y", h), (2, max(u, h), u), UNITS[u] * width(CHUNKS[h]) * 2.75e-3,
                lambda u=u, h=h: (tile(u, h), tile_out(u, h)),
            )
    for h in range(len(CHUNKS)):
        plan.task(
            ("pr", h), x_names(0) + ring_names("y", h) + ["parts_left"], (1, h),
            (UNITS[0] + 32) * width(CHUNKS[h]) * 2.75e-3,
            lambda h=h: (first_tile(h), left_out(h), tile_out(0, h)),
        )
        gathered = ring_names("p", h) if h < last else [("gp",), ("gp", 1)]
        plan.task(("r", h), gathered + [("pr", h), "map"], (1, 9), 0.3 * width(CHUNKS[h]), lambda h=h: project(h))

    plan.run(LOG)
    p_out = pltpu.make_async_copy(p_all, p_hbm, local_sem.at[0])
    p_out.start()
    for sent in plan.sent:
        sent()
    p_out.wait()


LOG = None


def exchange(inputs, out_grads, om, psi):
    dma = pltpu.SemaphoreType.DMA
    n_u, n_h = len(UNITS), len(CHUNKS)
    anywhere = pl.BlockSpec(memory_space=pl.ANY)
    local = pl.BlockSpec(memory_space=pltpu.VMEM)
    return pl.pallas_call(
        exchange_kernel,
        name="exchange",
        out_shape=(
            jax.ShapeDtypeStruct((BLOCK, RY), F32),
            jax.ShapeDtypeStruct((RY, BLOCK), F32),
            jax.ShapeDtypeStruct((2, 8, 16, BLOCK), F32),
            jax.ShapeDtypeStruct((BLOCK, BLOCK), F32),
        ),
        in_specs=[pl.BlockSpec(memory_space=pltpu.HBM)] * 4,
        out_specs=(local, local, anywhere, anywhere),
        scratch_shapes=[
            pltpu.VMEM((4, 4, BLOCK, TOK), BF16),
            pltpu.VMEM((16, TOK, BLOCK), BF16),
            pltpu.VMEM((4, 4, 2, 8, 16, RY), F32),
            pltpu.VMEM((16, 16, TOK), F32),
            pltpu.VMEM((16, 48, TOK), BF16),
            pltpu.VMEM((16, TOK, 3 * RY), BF16),
            pltpu.VMEM((BLOCK, BLOCK), F32),
            pltpu.VMEM((2, 8, 16, BLOCK), F32),
            pltpu.VMEM((16, 16, RY), F32),
            pltpu.VMEM((RY, RZ), F32),
            pltpu.VMEM((TOK, BLOCK), BF16),
            pltpu.VMEM((BLOCK, RY), F32),
            pltpu.VMEM((RZ, BLOCK), F32),
            pltpu.VMEM((16, 16, TOK), F32),
            pltpu.VMEM((16, 16, RY), F32),
            pltpu.VMEM((8, 16, TOK), F32),
            pltpu.VMEM((8, 16, TOK), F32),
            pltpu.VMEM((16, 16, RY), F32),
            pltpu.VMEM((RY, RY), F32),
            dma((2, 16)), dma((2, 16)),
            dma((16,)), dma((16,)),
            dma((8,)), dma((8,)),
            dma((16,)), dma((16,)),
            dma((16,)), dma((16,)),
            dma((n_u, 2, 15)), dma((n_u, 2, 15)),
            dma((4, 2, 3)), dma((4, 2, 3)),
            dma((4, 2, 3)), dma((4, 2, 3)),
            dma((n_h, 2, 4)), dma((n_h, 2, 4)),
            dma((n_h, 2, 5)), dma((n_h, 2, 5)),
            dma((n_h, 2, 4)), dma((n_h, 2, 4)),
            dma((n_h, 2, 5)), dma((n_h, 2, 5)),
            dma, dma, dma((4,)), dma((n_u, n_h)),
        ],
        compiler_params=pltpu.CompilerParams(
            collective_id=0, has_side_effects=True, vmem_limit_bytes=EXCHANGE_LIMIT * 1024 * 1024
        ),
    )(inputs, out_grads, om, psi)


def finish_kernel(g_ref, q_ref, r_ref, p_ref, res_ref, qo_ref, po_ref):
    q_high, q_low = split(q_ref[...], 2)
    r_high, r_low = split(r_ref[...], 2)
    left = jnp.concatenate([q_high, q_low, q_high], axis=1)
    right = jnp.concatenate([r_high, r_high, r_low], axis=0)
    res_ref[...] = g_ref[...] - dot(left, right)
    po_ref[...] = p_ref[...]

    @pl.when(pl.program_id(0) == 0)
    def _():
        qo_ref[...] = q_ref[...]


def finish(g, q, r, p):
    def cols(height):
        return pl.BlockSpec((height, FINISH_COLS), lambda i: (0, i))

    whole = pl.BlockSpec((BLOCK, RY), lambda i: (0, 0))
    return pl.pallas_call(
        finish_kernel,
        name="finish",
        grid=(BLOCK // FINISH_COLS,),
        out_shape=(
            jax.ShapeDtypeStruct((BLOCK, BLOCK), F32),
            jax.ShapeDtypeStruct((BLOCK, RY), F32),
            jax.ShapeDtypeStruct((RZ, BLOCK), F32),
        ),
        in_specs=[cols(BLOCK), whole, cols(RY), cols(RZ)],
        out_specs=(cols(BLOCK), whole, cols(RZ)),
        compiler_params=pltpu.CompilerParams(vmem_limit_bytes=FINISH_LIMIT * 1024 * 1024),
    )(g, q, r, p)


def per_device(inputs, out_grads, range_test, corange_test):
    q, r, p, g = exchange(inputs, out_grads, range_test, corange_test)
    residual, q, p = finish(g, q, r, p.reshape(RZ, BLOCK))
    return (q, p, residual)


def solution(mesh):
    placed = (P("col", "row"), P("row", "col"), P("col", None), P(None, "row"))
    return jax.shard_map(
        per_device,
        mesh=mesh,
        in_specs=placed,
        out_specs=(P("row", None), P(None, "col"), P("row", "col")),
        check_vma=False,
    )
```

```python
import heapq

import jax
import jax.numpy as jnp
from jax import lax
from jax.experimental import pallas as pl
from jax.experimental.pallas import tpu as pltpu
from jax.sharding import PartitionSpec as P

F32 = jnp.float32
BF16 = jnp.bfloat16
HIGHEST = lax.Precision.HIGHEST
MESH = pl.DeviceIdType.MESH

BLOCK = 1152
TOK = 256
RY = 128
RZ = 256
UNITS = (576, 576)
CHUNKS = (512, 512, 128)
FINISH_COLS = 384
EXCHANGE_LIMIT, FINISH_LIMIT = 42, 18

LINK_RATE = 46500.0
PARTNER_RATE = 150000.0
HOP = 1.6
SLACK = 2.5


def starts(sizes):
    return [sum(sizes[:i]) for i in range(len(sizes))]


UNIT_AT = starts(UNITS)
CHUNK_AT = starts(CHUNKS)


def dot(left_side, right_side, precision=None):
    return jnp.dot(left_side, right_side, precision=precision, preferred_element_type=F32)


def split(value, parts):
    out = []
    for _ in range(parts):
        piece = value.astype(BF16)
        value = value - piece.astype(F32)
        out.append(piece)
    return out


class Message:
    def __init__(self, name, loads, order, start, wait, then=None, sent=None, latency=HOP):
        self.name, self.loads, self.order = name, loads, order
        self.start, self.wait, self.then, self.sent, self.latency = start, wait, then, sent, latency


class Plan:
    def __init__(self):
        self.now, self.free, self.queues = 0.0, {}, {}
        self.flying, self.count, self.done, self.tasks, self.sent = [], 0, set(), [], []

    def post(self, message):
        self.count += 1
        link = next(iter(message.loads))
        heapq.heappush(self.queues.setdefault(link, []), (message.order, self.count, message))

    def launch(self, message):
        message.start()
        self.now += 0.03
        end = self.now
        for link, cost in message.loads.items():
            self.free[link] = max(self.now, self.free.get(link, 0.0)) + cost
            end = max(end, self.free[link])
        self.count += 1
        heapq.heappush(self.flying, (end + message.latency, self.count, message))
        if message.sent:
            self.sent.append(message.sent)

    def poll(self):
        for link, queue in self.queues.items():
            while queue and self.free.get(link, 0.0) - self.now < SLACK:
                self.launch(heapq.heappop(queue)[2])

    def task(self, name, needs, order, cost, run):
        self.tasks.append((order, len(self.tasks), name, frozenset(needs), cost, run))

    def finish(self, name):
        self.done.add(name)

    def run(self, log=None):
        while True:
            self.poll()
            if self.flying and self.flying[0][0] <= self.now:
                message = heapq.heappop(self.flying)[2]
                message.wait()
                if log is not None:
                    log.append((round(self.now, 1), "recv", message.name))
                self.now += 0.03
                self.finish(message.name)
                if message.then:
                    message.then()
                continue
            ready = [task for task in self.tasks if task[3] <= self.done]
            if ready:
                best = min(ready)
                self.tasks.remove(best)
                if log is not None:
                    log.append((round(self.now, 1), "task", best[2]))
                best[5]()
                self.now += best[4]
                self.finish(best[2])
                continue
            if not self.flying:
                break
            self.now = self.flying[0][0]
        assert not self.tasks, [(task[2], task[3] - self.done) for task in self.tasks]


def exchange_kernel(
    x_hbm, y_hbm, om_hbm, psi_hbm,
    q_ref, r_ref, p_hbm, g_hbm,
    xt4, yf, wf, ar, ahl, whl, g_acc, p_all, c_all, map_ref,
    x_own, om, psi, a_part, w_part, a_pre, a_in, w_in, inv_ref,
    rs_send, rs_recv, ga_send, ga_recv, gw_send, gw_recv, gc_send, gc_recv, gp_send, gp_recv,
    x_send, x_recv, w_send, w_recv, wp_send, wp_recv,
    z_send, z_recv, yp_send, yp_recv, p_send, p_recv, pp_send, pp_recv,
    own_send, own_recv, local_sem, out_sem,
):
    row, col = lax.axis_index("row"), lax.axis_index("col")
    z, k = row // 2, row % 2
    x, y = col // 4, col % 4
    partner = row + 1 - 2 * k
    me_row = 8 * k + z

    loads_in = [
        pltpu.make_async_copy(x_hbm, x_own, local_sem.at[0]),
        pltpu.make_async_copy(y_hbm, yf.at[row], local_sem.at[1]),
        pltpu.make_async_copy(psi_hbm, psi, local_sem.at[2]),
        pltpu.make_async_copy(om_hbm, om, local_sem.at[3]),
    ]
    for copy in loads_in:
        copy.start()

    barrier = pltpu.get_barrier_semaphore()

    def greet(j, carry):
        pl.semaphore_signal(barrier, inc=1, device_id=((row + j) % 16, col), device_id_type=MESH)
        pl.semaphore_signal(barrier, inc=1, device_id=(row, (col + j) % 16), device_id_type=MESH)
        return carry

    lax.fori_loop(1, 16, greet, 0)

    def remote(source, target, send, recv, device):
        return pltpu.make_async_remote_copy(
            src_ref=source, dst_ref=target, send_sem=send, recv_sem=recv,
            device_id=device, device_id_type=MESH,
        )

    plan = Plan()

    def along(first_axis, step):
        if first_axis:
            return (row, ((x + step + 4) % 4) * 4 + y)
        return (row, x * 4 + (y + step + 4) % 4)

    def x_view(u, a, o1, o2):
        n = UNITS[u] // 2
        rows = pl.ds(UNIT_AT[u] + n * a, n)
        ox, oy = (o1, o2) if a == 0 else (o2, o1)
        return xt4.at[(x + ox + 4) % 4, (y + oy + 4) % 4, rows, :]

    def x_message(u, a, phase, o1, step, hop):
        on_x = (a == 0) == (phase == 0)
        link = ("x" if on_x else "y") + ("+" if step > 0 else "-")
        if phase == 0:
            slot = {(1, 1): 0, (-1, 1): 1}.get((step, hop), 2)
            out_o, in_o = (-step * (hop - 1), 0), (-step * hop, 0)
        else:
            slot = 3 + 3 * (o1 % 4) + {(1, 1): 0, (-1, 1): 1}.get((step, hop), 2)
            out_o, in_o = (o1, -step * (hop - 1)), (o1, -step * hop)
        here, there = x_view(u, a, *out_o), x_view(u, a, *in_o)
        send, recv = x_send.at[u, a, slot], x_recv.at[u, a, slot]
        name = ("x", u, a, slot)

        def start():
            remote(here, here, send, recv, along(on_x, step)).start()

        def wait():
            remote(there, there, send, recv, along(on_x, step)).wait_recv()

        def sent():
            remote(here, here, send, recv, along(on_x, step)).wait_send()

        def then():
            if phase == 0:
                far = 1 if (u + a) % 2 == 0 else -1
                if hop == 1 and step == far:
                    plan.post(x_message(u, a, 0, 0, step, 2))
                came = (-step * hop) % 4
                plan.post(x_message(u, a, 1, came, 1, 1))
                plan.post(x_message(u, a, 1, came, -1, 1))
            else:
                far = 1 if (o1 % 4 in (0, 2)) == ((u + a) % 2 == 0) else -1
                if hop == 1 and step == far:
                    plan.post(x_message(u, a, 1, o1, step, 2))

        cost = UNITS[u] // 2 * TOK * 2 / LINK_RATE
        return Message(name, {link: cost}, (1, u, phase), start, wait, then, sent)

    def x_names(u):
        return [("x", u, a, slot) for a in (0, 1) for slot in range(15)]

    def x_begin(u):
        for a in (0, 1):
            for phase in (0, 1):
                for step in (1, -1):
                    plan.post(x_message(u, a, phase, 0, step, 1))

    def ring_long(h, d):
        return (h % 2) == d

    def z_peer(step):
        return (2 * ((z + step + 8) % 8) + k, col)

    def y_view(h, offset, kk):
        return yf.at[2 * ((z + offset + 8) % 8) + kk, :, pl.ds(CHUNK_AT[h], CHUNKS[h])]

    def p_view(h, offset, kk):
        return p_all.at[kk, (z + offset + 8) % 8, :, pl.ds(CHUNK_AT[h], CHUNKS[h])]

    kinds = {
        "y": (y_view, z_send, z_recv, yp_send, yp_recv, TOK * 2, 1),
        "p": (p_view, p_send, p_recv, pp_send, pp_recv, 64, 0),
    }

    def partner_message(kind, h, d, s):
        view, _, _, send_sem, recv_sem, height, order = kinds[kind]
        offset = -s if d == 0 else s
        here, there = view(h, offset, k), view(h, offset, 1 - k)
        send, recv = send_sem.at[h, d, s], recv_sem.at[h, d, s]

        def start():
            remote(here, here, send, recv, (partner, col)).start()

        def wait():
            remote(there, there, send, recv, (partner, col)).wait_recv()

        def sent():
            remote(here, here, send, recv, (partner, col)).wait_send()

        cost = CHUNKS[h] * height / PARTNER_RATE
        return Message((kind + "p", h, d, s), {"p": cost}, (order, h), start, wait, None, sent)

    def ring_message(kind, h, d, s):
        view, send_sem, recv_sem, _, _, height, order = kinds[kind]
        step = 1 if d == 0 else -1
        here, there = view(h, -step * (s - 1), k), view(h, -step * s, k)
        send, recv = send_sem.at[h, d, s - 1], recv_sem.at[h, d, s - 1]

        def start():
            remote(here, here, send, recv, z_peer(step)).start()

        def wait():
            remote(there, there, send, recv, z_peer(step)).wait_recv()

        def sent():
            remote(here, here, send, recv, z_peer(step)).wait_send()

        def then():
            if s < 3 or (s == 3 and ring_long(h, d)):
                plan.post(ring_message(kind, h, d, s + 1))
            plan.post(partner_message(kind, h, d, s))

        cost = CHUNKS[h] * height / LINK_RATE
        return Message((kind, h, d, s), {"z+" if d == 0 else "z-": cost}, (order, h, s), start, wait, then, sent)

    def ring_begin(kind, h):
        plan.post(ring_message(kind, h, 0, 1))
        plan.post(ring_message(kind, h, 1, 1))
        plan.post(partner_message(kind, h, 0, 0))

    def ring_names(kind, h):
        names = [(kind + "p", h, 0, 0)]
        for d in (0, 1):
            for s in (1, 2, 3) + ((4,) if ring_long(h, d) else ()):
                names += [(kind, h, d, s), (kind + "p", h, d, s)]
        return names

    def w_view(v, phase, offset, kk):
        first, second = (x, y) if v < 2 else (y, x)
        if phase == 0:
            f, s = (first + offset + 4) % 4, second
        else:
            f, s = slice(None), (second + offset + 4) % 4
        xi, yi = (f, s) if v < 2 else (s, f)
        return wf.at[xi, yi, kk, pl.ds(2 * v, 2)]

    def w_partner(v, phase, j):
        offset = (-1, 1, 2)[j]
        here, there = w_view(v, phase, offset, k), w_view(v, phase, offset, 1 - k)
        send, recv = wp_send.at[v, phase, j], wp_recv.at[v, phase, j]

        def start():
            remote(here, here, send, recv, (partner, col)).start()

        def wait():
            remote(there, there, send, recv, (partner, col)).wait_recv()

        def sent():
            remote(here, here, send, recv, (partner, col)).wait_send()

        cost = 16384 * (4 if phase else 1) / PARTNER_RATE
        return Message(("wp", v, phase, j), {"p": cost}, (0,), start, wait, None, sent)

    def w_message(v, phase, j):
        far = 1 if v % 2 == 0 else -1
        step = (1, -1, far)[j]
        here, there = w_view(v, phase, (0, 0, -far)[j], k), w_view(v, phase, (-1, 1, 2)[j], k)
        send, recv = w_send.at[v, phase, j], w_recv.at[v, phase, j]
        on_x = (v < 2) == (phase == 0)
        link = ("x" if on_x else "y") + ("+" if step > 0 else "-")

        def start():
            remote(here, here, send, recv, along(on_x, step)).start()

        def wait():
            remote(there, there, send, recv, along(on_x, step)).wait_recv()

        def sent():
            remote(here, here, send, recv, along(on_x, step)).wait_send()

        def then():
            if j < 2 and step == far:
                plan.post(w_message(v, phase, 2))
            plan.post(w_partner(v, phase, j))

        cost = 16384 * (4 if phase else 1) / LINK_RATE
        return Message(("w", v, phase, j), {link: cost}, (0, phase), start, wait, then, sent)

    w_names = [(kind, v, phase, j) for kind in ("w", "wp") for v in range(4) for phase in (0, 1) for j in range(3)]

    loads_in[0].wait()
    xt4[x, y] = x_own[...].T
    loads_in[1].wait()
    pl.semaphore_wait(barrier, 30)
    for u in range(len(UNITS)):
        x_begin(u)
    for h in range(len(CHUNKS)):
        ring_begin("y", h)
    plan.poll()

    loads_in[2].wait()
    loads_in[3].wait()

    def own_left(i, carry):
        rows = pl.ds(pl.multiple_of(i * 128, 128), 128)
        parts = jnp.concatenate(split(psi[rows, :], 3), axis=0)
        both = dot(parts, xt4[x, y])
        total = both[0:128] + both[128:256] + both[256:384]
        a_part[pl.ds(pl.multiple_of(i * 8, 8), 8)] = total.reshape(8, 16, TOK)
        return carry

    lax.fori_loop(0, 2, own_left, 0)
    parts = jnp.concatenate(split(om[...], 3), axis=1)
    both = dot(yf[row], parts)
    w_part[...] = (both[:, 0:128] + both[:, 128:256] + both[:, 256:384]).reshape(16, 16, RY)
    plan.now += 4.0

    def loop_row(run):
        def body(j, carry):
            run((row + j) % 16)
            return carry

        lax.fori_loop(1, 16, body, 0)

    def loop_col(run):
        def body(j, carry):
            run((col + j) % 16)
            return carry

        lax.fori_loop(1, 16, body, 0)

    def slot_of(t):
        return 8 * (t % 2) + t // 2

    mine = pl.ds(pl.multiple_of(8 * k, 8), 8)
    theirs = pl.ds(pl.multiple_of(8 * (1 - k), 8), 8)

    def loop_z(run):
        def body(j, carry):
            run((z + j) % 8)
            return carry

        lax.fori_loop(1, 8, body, 0)

    pre_out = remote(a_part.at[theirs], a_pre, rs_send.at[0, 8], rs_recv.at[0, 8], (partner, col))

    def rs_left(t):
        return remote(a_part.at[8 * k + t], a_in.at[z], rs_send.at[0, t], rs_recv.at[0, z], (2 * t + k, col))

    def rs_left_in(t):
        return remote(a_in.at[t], a_in.at[t], rs_send.at[0, t], rs_recv.at[0, t], (2 * t + k, col))

    def rs_right(c):
        return remote(w_part.at[c], w_in.at[col], rs_send.at[1, c], rs_recv.at[1, col], (row, c))

    def rs_right_in(c):
        return remote(w_in.at[c], w_in.at[c], rs_send.at[1, c], rs_recv.at[1, c], (row, c))

    plan.launch(Message(
        ("rs", 1), {link: 1.4 for link in ("x+", "x-", "y+", "y-")}, (0,),
        lambda: loop_col(lambda c: rs_right(c).start()), lambda: loop_col(lambda c: rs_right_in(c).wait_recv()),
        None, lambda: loop_col(lambda c: rs_right(c).wait_send()), 3.5,
    ))
    plan.launch(Message(
        ("pre",), {"p": 0.9}, (0,), pre_out.start, pre_out.wait_recv, None, pre_out.wait_send
    ))

    def scatter_left():
        a_part[mine] = a_part[mine] + a_pre[...]
        plan.launch(Message(
            ("rs", 0), {link: 2.8 for link in ("z+", "z-")}, (0,),
            lambda: loop_z(lambda t: rs_left(t).start()), lambda: loop_z(lambda t: rs_left_in(t).wait_recv()),
            None, lambda: loop_z(lambda t: rs_left(t).wait_send()), 3.5,
        ))

    plan.task("scatter_left", [("pre",)], (0,), 0.3, scatter_left)

    def ga(c):
        return remote(ar.at[col], ar.at[col], ga_send.at[c], ga_recv.at[col], (row, c))

    def ga_in(c):
        return remote(ar.at[c], ar.at[c], ga_send.at[c], ga_recv.at[c], (row, c))

    def gw(t):
        here = wf.at[x, y, k, z]
        return remote(here, here, gw_send.at[t], gw_recv.at[z], (2 * t + k, col))

    def gw_in(t):
        there = wf.at[x, y, k, t]
        return remote(there, there, gw_send.at[t], gw_recv.at[t], (2 * t + k, col))

    def spread(name, cost, piece, whole, send_sem, recv_sem):
        def out(t):
            return remote(piece(z), piece(z), send_sem.at[t], recv_sem.at[z], (2 * t + k, col))

        def into(t):
            return remote(piece(t), piece(t), send_sem.at[t], recv_sem.at[t], (2 * t + k, col))

        half = remote(whole(k), whole(k), send_sem.at[8], recv_sem.at[8], (partner, col))
        other = remote(whole(1 - k), whole(1 - k), send_sem.at[8], recv_sem.at[8], (partner, col))
        plan.launch(Message(
            (name,), {"z+": cost, "z-": cost}, (0,),
            lambda: loop_z(lambda t: out(t).start()), lambda: loop_z(lambda t: into(t).wait_recv()),
            lambda: plan.post(Message(
                (name, 1), {"p": 0.4}, (0,), half.start, other.wait_recv, None, half.wait_send
            )),
            lambda: loop_z(lambda t: out(t).wait_send()), 3.5,
        ))

    last = len(CHUNKS) - 1
    last_cols = pl.ds(CHUNK_AT[last], CHUNKS[last])

    own_half = wf.at[x, y, k]
    their_half = wf.at[x, y, 1 - k]
    half_out = remote(own_half, own_half, own_send, own_recv, (partner, col))
    half_in = remote(their_half, their_half, own_send, own_recv, (partner, col))

    def reduce_right():
        total = lax.fori_loop(1, 16, lambda j, sum_now: sum_now + w_in[(col + j) % 16], w_part[col])
        wf[x, y, k, z] = total

    def reduce_left():
        total = lax.fori_loop(1, 8, lambda j, sum_now: sum_now + a_in[(z + j) % 8], a_part[me_row])
        ar[col] = total

    def send_right():
        plan.launch(Message(
            ("gw",), {"z+": 1.4, "z-": 1.4}, (0,),
            lambda: loop_z(lambda t: gw(t).start()), lambda: loop_z(lambda t: gw_in(t).wait_recv()),
            w_ring, lambda: loop_z(lambda t: gw(t).wait_send()), 3.5,
        ))

    def w_ring():
        for v in range(4):
            for phase in (0,):
                plan.post(w_message(v, phase, 0))
                plan.post(w_message(v, phase, 1))
        plan.post(Message(("wh",), {"p": 0.5}, (0,), half_out.start, half_in.wait_recv, None, half_out.wait_send))

    def send_left():
        plan.launch(Message(
            ("ga",), {link: 2.8 for link in ("x+", "x-", "y+", "y-")}, (0,),
            lambda: loop_col(lambda c: ga(c).start()), lambda: loop_col(lambda c: ga_in(c).wait_recv()),
            None, lambda: loop_col(lambda c: ga(c).wait_send()), 3.5,
        ))

    plan.task("reduce_right", [("rs", 1)], (0,), 0.4, lambda: (reduce_right(), send_right()))
    plan.task("reduce_left", [("rs", 0)], (0,), 0.4, lambda: (reduce_left(), send_left()))
    for v in range(4):
        plan.task(
            ("line", v), [("w", v, 0, j) for j in range(3)], (0,), 0.0,
            lambda v=v: (plan.post(w_message(v, 1, 0)), plan.post(w_message(v, 1, 1))),
        )

    def parts_left():
        for b in range(16):
            ahl[b] = jnp.concatenate(split(ar[b], 3), axis=0)

    def parts_right(quarter):
        def body(i, carry):
            b = quarter * 4 + i
            whl[b] = jnp.concatenate(split(wf[:, :, b % 2, b // 2].reshape(TOK, RY), 3), axis=1)
            return carry

        lax.fori_loop(0, 4, body, 0)

    def left_rows(parts):
        return jnp.concatenate([ahl[b, 0:16 * parts, :] for b in range(16)], axis=1)

    def core_rows():
        both = dot(left_rows(3), whl[...].reshape(16 * TOK, 3 * RY))
        total = both[0:16] + both[16:32] + both[32:48]
        c_all[me_row] = total[:, 0:RY] + total[:, RY:2 * RY] + total[:, 2 * RY:]

    def send_core():
        spread(
            "gc", 1.4, lambda t: c_all.at[8 * k + t],
            lambda kk: c_all.at[pl.ds(pl.multiple_of(8 * kk, 8), 8)], gc_send, gc_recv,
        )

    plan.task("parts_left", [("ga",)], (1,), 0.3, parts_left)
    needs_w = w_names + [("wh",), ("gw",)]
    for quarter in range(4):
        plan.task(("parts", quarter), needs_w, (0, 1), 0.3, lambda quarter=quarter: parts_right(quarter))
    all_parts = ["parts_left"] + [("parts", quarter) for quarter in range(4)]
    plan.task("core_rows", all_parts, (0, 2), 1.0, lambda: (core_rows(), send_core()))

    def core_t():
        return c_all[...].reshape(RZ, RY).T

    def gram():
        inv_ref[...] = dot(core_t(), c_all[...].reshape(RZ, RY), HIGHEST)

    def pivots(begin):
        lanes = lax.broadcasted_iota(jnp.int32, (RY, RY), 1)
        subs = lax.broadcasted_iota(jnp.int32, (RY, RY), 0)

        def pivot(step, carry):
            i = 2 * step
            now = inv_ref[...]
            line_a = inv_ref[pl.ds(i, 1), :]
            line_b = inv_ref[pl.ds(i + 1, 1), :]
            at_a, at_b = lanes == i, lanes == i + 1
            on_a, on_b = subs == i, subs == i + 1

            def pick(mask, value):
                return jnp.sum(jnp.where(mask, value, 0.0), axis=1, keepdims=True)

            over_a, over_b = pick(at_a, now), pick(at_b, now)
            aa, ab = pick(at_a[0:1], line_a), pick(at_b[0:1], line_a)
            ba, bb = pick(at_a[0:1], line_b), pick(at_b[0:1], line_b)
            head = 1.0 / aa
            ratio_a, ratio_b = ba * head, ab * head
            rest = 1.0 / (bb - ba * ratio_b)
            low, high = -ratio_a * rest, -ratio_b * rest
            top = head + ratio_b * rest * ratio_a
            row_a = top * line_a + high * line_b
            row_b = low * line_a + rest * line_b
            col_a = over_a * top + over_b * low
            col_b = over_a * high + over_b * rest
            inner = now - over_a * row_a - over_b * row_b
            inner = jnp.where(at_a, -col_a, jnp.where(at_b, -col_b, inner))
            row_a = jnp.where(at_a[0:1], top, jnp.where(at_b[0:1], high, row_a))
            row_b = jnp.where(at_a[0:1], low, jnp.where(at_b[0:1], rest, row_b))
            inv_ref[...] = jnp.where(on_a, row_a, jnp.where(on_b, row_b, inner))
            return carry

        lax.fori_loop(begin // 2, begin // 2 + 8, pivot, 0)

    def core_map():
        map_ref[...] = dot(inv_ref[...], core_t(), HIGHEST)

    plan.task("gram", [("gc",), ("gc", 1)], (0, 3), 0.7, gram)
    before = "gram"
    for begin in range(0, RY, 16):
        plan.task(("pivots", begin), [before], (0, 4), 0.7, lambda begin=begin: pivots(begin))
        before = ("pivots", begin)
    plan.task("map", [before], (0, 5), 0.6, core_map)

    def unit_rows(u):
        rows = pl.ds(UNIT_AT[u], UNITS[u])
        return jnp.concatenate([xt4[b // 4, b % 4, rows, :] for b in range(16)], axis=1)

    def right_product(u):
        both = dot(unit_rows(u), whl[:, :, 0:2 * RY].reshape(16 * TOK, 2 * RY))
        q_ref[pl.ds(UNIT_AT[u], UNITS[u]), :] = both[:, 0:RY] + both[:, RY:]

    def chunk(h):
        return yf[:, :, pl.ds(CHUNK_AT[h], CHUNKS[h])].reshape(16 * TOK, CHUNKS[h])

    def g_out(u, h):
        at = (pl.ds(UNIT_AT[u], UNITS[u]), pl.ds(CHUNK_AT[h], CHUNKS[h]))
        return pltpu.make_async_copy(g_acc.at[at], g_hbm.at[at], out_sem.at[u, h])

    def tile(u, h):
        g_acc[pl.ds(UNIT_AT[u], UNITS[u]), pl.ds(CHUNK_AT[h], CHUNKS[h])] = dot(unit_rows(u), chunk(h))

    def first_tile(h):
        cols = pl.ds(CHUNK_AT[h], CHUNKS[h])
        both = dot(jnp.concatenate([unit_rows(0), left_rows(2)], axis=0), chunk(h))
        g_acc[pl.ds(0, UNITS[0]), cols] = both[0:UNITS[0]]
        p_all[k, z, :, cols] = both[UNITS[0]:UNITS[0] + 16] + both[UNITS[0] + 16:]

    def tile_out(u, h):
        g_out(u, h).start()
        plan.sent.append(lambda: g_out(u, h).wait())

    def left_out(h):
        if h < last:
            ring_begin("p", h)
        else:
            spread(
                "gp", 1.4, lambda t: p_all.at[k, t, :, last_cols],
                lambda kk: p_all.at[kk, :, :, last_cols], gp_send, gp_recv,
            )

    def project(h):
        cols = pl.ds(CHUNK_AT[h], CHUNKS[h])
        r_ref[:, cols] = dot(map_ref[...], p_all[:, :, :, cols].reshape(RZ, CHUNKS[h]), HIGHEST)

    def width(n):
        return (n + 255) // 256

    for u in range(len(UNITS)):
        plan.task(("q", u), x_names(u) + all_parts, (3, u), UNITS[u] * 2.75e-3, lambda u=u: right_product(u))
        for h in range(len(CHUNKS)) if u else ():
            plan.task(
                ("g", u, h), x_names(u) + ring_names("y", h), (2, max(u, h), u), UNITS[u] * width(CHUNKS[h]) * 2.75e-3,
                lambda u=u, h=h: (tile(u, h), tile_out(u, h)),
            )
    for h in range(len(CHUNKS)):
        plan.task(
            ("pr", h), x_names(0) + ring_names("y", h) + ["parts_left"], (1, h),
            (UNITS[0] + 32) * width(CHUNKS[h]) * 2.75e-3,
            lambda h=h: (first_tile(h), left_out(h), tile_out(0, h)),
        )
        gathered = ring_names("p", h) if h < last else [("gp",), ("gp", 1)]
        plan.task(("r", h), gathered + [("pr", h), "map"], (1, 9), 0.3 * width(CHUNKS[h]), lambda h=h: project(h))

    plan.run(LOG)
    p_out = pltpu.make_async_copy(p_all, p_hbm, local_sem.at[0])
    p_out.start()
    for sent in plan.sent:
        sent()
    p_out.wait()


LOG = None


def exchange(inputs, out_grads, om, psi):
    dma = pltpu.SemaphoreType.DMA
    n_u, n_h = len(UNITS), len(CHUNKS)
    anywhere = pl.BlockSpec(memory_space=pl.ANY)
    local = pl.BlockSpec(memory_space=pltpu.VMEM)
    return pl.pallas_call(
        exchange_kernel,
        name="exchange",
        out_shape=(
            jax.ShapeDtypeStruct((BLOCK, RY), F32),
            jax.ShapeDtypeStruct((RY, BLOCK), F32),
            jax.ShapeDtypeStruct((2, 8, 16, BLOCK), F32),
            jax.ShapeDtypeStruct((BLOCK, BLOCK), F32),
        ),
        in_specs=[pl.BlockSpec(memory_space=pltpu.HBM)] * 4,
        out_specs=(local, local, anywhere, anywhere),
        scratch_shapes=[
            pltpu.VMEM((4, 4, BLOCK, TOK), BF16),
            pltpu.VMEM((16, TOK, BLOCK), BF16),
            pltpu.VMEM((4, 4, 2, 8, 16, RY), F32),
            pltpu.VMEM((16, 16, TOK), F32),
            pltpu.VMEM((16, 48, TOK), BF16),
            pltpu.VMEM((16, TOK, 3 * RY), BF16),
            pltpu.VMEM((BLOCK, BLOCK), F32),
            pltpu.VMEM((2, 8, 16, BLOCK), F32),
            pltpu.VMEM((16, 16, RY), F32),
            pltpu.VMEM((RY, RZ), F32),
            pltpu.VMEM((TOK, BLOCK), BF16),
            pltpu.VMEM((BLOCK, RY), F32),
            pltpu.VMEM((RZ, BLOCK), F32),
            pltpu.VMEM((16, 16, TOK), F32),
            pltpu.VMEM((16, 16, RY), F32),
            pltpu.VMEM((8, 16, TOK), F32),
            pltpu.VMEM((8, 16, TOK), F32),
            pltpu.VMEM((16, 16, RY), F32),
            pltpu.VMEM((RY, RY), F32),
            dma((2, 16)), dma((2, 16)),
            dma((16,)), dma((16,)),
            dma((8,)), dma((8,)),
            dma((16,)), dma((16,)),
            dma((16,)), dma((16,)),
            dma((n_u, 2, 15)), dma((n_u, 2, 15)),
            dma((4, 2, 3)), dma((4, 2, 3)),
            dma((4, 2, 3)), dma((4, 2, 3)),
            dma((n_h, 2, 4)), dma((n_h, 2, 4)),
            dma((n_h, 2, 5)), dma((n_h, 2, 5)),
            dma((n_h, 2, 4)), dma((n_h, 2, 4)),
            dma((n_h, 2, 5)), dma((n_h, 2, 5)),
            dma, dma, dma((4,)), dma((n_u, n_h)),
        ],
        compiler_params=pltpu.CompilerParams(
            collective_id=0, has_side_effects=True, vmem_limit_bytes=EXCHANGE_LIMIT * 1024 * 1024
        ),
    )(inputs, out_grads, om, psi)


def finish_kernel(g_ref, q_ref, r_ref, p_ref, res_ref, qo_ref, po_ref):
    q_high, q_low = split(q_ref[...], 2)
    r_high, r_low = split(r_ref[...], 2)
    left = jnp.concatenate([q_high, q_low, q_high], axis=1)
    right = jnp.concatenate([r_high, r_high, r_low], axis=0)
    res_ref[...] = g_ref[...] - dot(left, right)
    po_ref[...] = p_ref[...]

    @pl.when(pl.program_id(0) == 0)
    def _():
        qo_ref[...] = q_ref[...]


def finish(g, q, r, p):
    def cols(height):
        return pl.BlockSpec((height, FINISH_COLS), lambda i: (0, i))

    whole = pl.BlockSpec((BLOCK, RY), lambda i: (0, 0))
    return pl.pallas_call(
        finish_kernel,
        name="finish",
        grid=(BLOCK // FINISH_COLS,),
        out_shape=(
            jax.ShapeDtypeStruct((BLOCK, BLOCK), F32),
            jax.ShapeDtypeStruct((BLOCK, RY), F32),
            jax.ShapeDtypeStruct((RZ, BLOCK), F32),
        ),
        in_specs=[cols(BLOCK), whole, cols(RY), cols(RZ)],
        out_specs=(cols(BLOCK), whole, cols(RZ)),
        compiler_params=pltpu.CompilerParams(vmem_limit_bytes=FINISH_LIMIT * 1024 * 1024),
    )(g, q, r, p)


def per_device(inputs, out_grads, range_test, corange_test):
    q, r, p, g = exchange(inputs, out_grads, range_test, corange_test)
    residual, q, p = finish(g, q, r, p.reshape(RZ, BLOCK))
    return (q, p, residual)


def solution(mesh):
    placed = (P("col", "row"), P("row", "col"), P("col", None), P(None, "row"))
    return jax.shard_map(
        per_device,
        mesh=mesh,
        in_specs=placed,
        out_specs=(P("row", None), P(None, "col"), P("row", "col")),
        check_vma=False,
    )
```
